128 devices in a mesh: seq: 16 (over y_lo, x, core), head: 8 (over y_hi, z).
Axes of the slice: x: 4, y: 4 (y_hi: 2, y_lo: 2; y = y_hi * 2 + y_lo), z: 4, core: 2. Of those that a mesh axis runs over, the one named last changes fastest.
Arguments:
- video_in: bfloat16 [10240, 3072], P('seq'), may hold values from -6 to 6
- text_in: bfloat16 [256, 3072], P('seq'), may hold values from -6 to 6
- mod_video: float32 [3, 3072], replicated, may hold values from -4 to 4
- mod_text: float32 [3, 3072], replicated, may hold values from -4 to 4
- qkv_video: bfloat16 [3072, 3, 3072], P('seq', None, 'head'), may hold values from -0.109375 to 0.109375
- qkv_text: bfloat16 [3072, 3, 3072], P('seq', None, 'head'), may hold values from -0.109375 to 0.109375
- proj_video: bfloat16 [3072, 3072], P('head', 'seq'), may hold values from -0.15625 to 0.15625
- proj_text: bfloat16 [3072, 3072], P('head', 'seq'), may hold values from -0.15625 to 0.15625
- gain_video: float32 [2, 128], replicated, may hold values from 1.5 to 12
- gain_text: float32 [2, 128], replicated, may hold values from 1.5 to 12
- windows: int32 [24, 3], replicated, may hold values from 0 to 4, as said below
- text_len: int32 [1], replicated, may hold values from 64 to 256
Outputs:
- video_out: bfloat16 [10240, 3072], P('seq', 'head')
- text_out: bfloat16 [256, 3072], P('seq', 'head')
The draws below stay inside these ranges and needn't reach their ends.
Inputs may be any that keep to these rules, and one draw needn't show every extreme that they name: `windows`: row h holds head h's half-widths: time tiles 0 to 1, height tiles 0 to 1, width tiles 0 to 4; some head has all three at their largest.
All inputs are finite; a program needn't handle non-finite values.
Results may differ from the reference program's by a relative error of at most 0.014.
The reference program's roundings to bfloat16 on the way count: a program that leaves them out, or rounds other values in their place, can miss the bound.
Values may be sent and summed in bfloat16 or wider, within the bound.
A program may use at most 128 MiB of HBM per device.

```python
import math
import jax
import jax.numpy as jnp
from jax import lax

D = 3072
HEADS = 24
HD = 128
FRAMES = 4
TT = 2
TH = 4
TW = 16
W = 80
HT_DEV = 1
TEXT = 256
VIDEO = 10240
N_SEQ = 16


def gain_values(key):
    uniform_part = jax.random.uniform(key, (2, HD), jnp.float32)
    return jnp.exp(math.log(1.5) + (math.log(3.5) - math.log(1.5)) * uniform_part)


def draw_gain_video(key, part):
    return gain_values(jax.random.fold_in(key, 11))


def draw_gain_text(key, part):
    return gain_values(jax.random.fold_in(key, 12))


def draw_windows(key, part):
    keys_all = jax.random.split(jax.random.fold_in(key, 13), 4)
    time_span = jax.random.randint(keys_all[0], (HEADS,), 0, FRAMES // TT)
    height_span = jax.random.randint(keys_all[1], (HEADS,), 0, HT_DEV + 1)
    width_span = jax.random.randint(keys_all[2], (HEADS,), 0, W // TW)
    chosen = jax.random.randint(keys_all[3], (), 0, HEADS)
    widest = jnp.arange(HEADS) == chosen
    time_span = jnp.where(widest, FRAMES // TT - 1, time_span)
    height_span = jnp.where(widest, HT_DEV, height_span)
    width_span = jnp.where(widest, W // TW - 1, width_span)
    return jnp.stack([time_span, height_span, width_span], 1).astype(jnp.int32)


def raised(values, rng, source, target, parts, factor):
    def block_of(position):
        return (jnp.arange(values.shape[position]) // (values.shape[position] // parts)).reshape((-1,) + (1,) * (values.ndim - 1 - position))

    first = jax.random.permutation(rng, parts)[block_of(target)]
    second = (block_of(target) + parts // 2) % parts
    return jnp.where((block_of(source) == first) | (block_of(source) == second), factor * values, values)


def levels(stream_key, dims, cuts, least, high):
    level, own = 1.0, jax.random.fold_in(stream_key, 6)
    for dim, blocks in cuts:
        heights = jnp.exp(jax.random.uniform(jax.random.fold_in(own, dim), (blocks,), jnp.float32, least / len(cuts), high / len(cuts)))
        level = level * jnp.repeat(heights, dims[dim] // blocks).reshape([-1 if axis == dim else 1 for axis in range(len(dims))])
    return level


def centred(own_key, extent, scale, reach, pieces=(), kind=jnp.bfloat16):
    drawn = scale * jax.random.normal(own_key, extent, jnp.float32)
    if pieces:
        drawn = drawn * levels(own_key, extent, pieces, -0.22, 0.18)
    return jnp.clip(drawn, -reach, reach).astype(kind)


def bell_draw_with(stream_key, shape, width, bound, shards, heavy, kind=jnp.bfloat16):
    values = width * jax.random.normal(stream_key, shape, jnp.float32)
    if shards:
        values = values * levels(stream_key, shape, shards, -0.22, 0.18)
    return jnp.clip(raised(values, jax.random.fold_in(stream_key, 3), *heavy), -bound, bound).astype(kind)


def setup_inputs(seed: int = 0) -> dict:
    seeds = jax.random.split(jax.random.key(seed), 13)
    video_in = centred(seeds[0], (VIDEO, D), 1.0, 6.0, ((0, 16),))
    text_in = centred(seeds[1], (TEXT, D), 1.0, 6.0, ((0, 16),))
    mod_video = centred(seeds[2], (3, D), 0.6, 4.0, (), jnp.float32)
    mod_text = centred(seeds[3], (3, D), 0.6, 4.0, (), jnp.float32)
    qkv_video = centred(seeds[4], (D, 3, D), D ** -0.5, 0.109375, ((0, 16), (2, 8)))
    qkv_text = centred(seeds[5], (D, 3, D), D ** -0.5, 0.109375, ((0, 16), (2, 8)))
    proj_video = bell_draw_with(seeds[6], (D, D), D ** -0.5, 0.15625, ((0, 8), (1, 16)), (0, 1, 16, 2.0))
    proj_text = bell_draw_with(seeds[7], (D, D), D ** -0.5, 0.15625, ((0, 8), (1, 16)), (0, 1, 16, 2.0))
    gain_video = draw_gain_video(jax.random.fold_in(seeds[12], 71), 0)
    gain_text = draw_gain_text(jax.random.fold_in(seeds[12], 71), 0)
    windows = draw_windows(jax.random.fold_in(seeds[12], 71), 0)
    text_len = jax.random.randint(seeds[11], (1,), TEXT // 4, TEXT + 1).astype(jnp.int32)
    return dict(video_in=video_in, text_in=text_in, mod_video=mod_video, mod_text=mod_text, qkv_video=qkv_video, qkv_text=qkv_text, proj_video=proj_video, proj_text=proj_text, gain_video=gain_video, gain_text=gain_text, windows=windows, text_len=text_len)


NEG_BIG = -1e+30

def modulate(tokens, modulation):
    values = tokens.astype(jnp.float32)
    center = lax.optimization_barrier(jnp.mean(values, axis=1, keepdims=True))
    spread = lax.optimization_barrier(jnp.mean(jnp.square(values - center), axis=1, keepdims=True))
    normed = (values - center) * lax.rsqrt(spread + 1e-06)
    return (normed * (1.0 + modulation[1]) + modulation[0]).astype(jnp.bfloat16)

def head_norm(values, gains_row):
    row_count = values.shape[0]
    by_head = values.reshape(row_count, -1, HD)
    scaled = by_head * lax.rsqrt(lax.optimization_barrier(jnp.mean(jnp.square(by_head), axis=2, keepdims=True)) + 1e-06) * gains_row
    return scaled.reshape(row_count, -1).astype(jnp.bfloat16)

def finish_qkv(projected, gains):
    return (head_norm(projected[:, 0], gains[0]), head_norm(projected[:, 1], gains[1]), projected[:, 2].astype(jnp.bfloat16))

def tile_coords(block_index, row_count, hblocks):
    positions = jnp.arange(row_count, dtype=jnp.int32)
    t_tile = jnp.zeros((row_count,), jnp.int32) + block_index // hblocks
    h_tile = block_index % hblocks * HT_DEV + positions % (HT_DEV * TH * W) // (W * TH)
    w_tile = positions % W // TW
    return (t_tile, h_tile, w_tile)

def window_mask(query_pos, key_pos, spans):
    inside_all = None
    for number in range(3):
        distance = jnp.abs(query_pos[number][:, None] - key_pos[number][None, :])
        inside = distance[None, :, :] <= spans[:, number][:, None, None]
        inside_all = inside if inside_all is None else inside_all & inside
    return inside_all

def softmax_attend(queries, key_vecs, value_vecs, allowed):
    scores = jnp.einsum('qhd,khd->hqk', queries.astype(jnp.float32), key_vecs.astype(jnp.float32)) * HD ** (-0.5)
    scores = jnp.where(allowed, scores, NEG_BIG)
    row_max = lax.optimization_barrier(jnp.max(scores, axis=2, keepdims=True))
    powers = jnp.where(allowed, jnp.exp(scores - row_max), 0.0)
    row_sum = lax.optimization_barrier(jnp.sum(powers, axis=2))
    probs = lax.optimization_barrier(powers.astype(jnp.bfloat16)).astype(jnp.float32)
    summed = jnp.einsum('hqk,khd->hqd', probs, value_vecs.astype(jnp.float32))
    result = summed / row_sum[:, :, None]
    return jnp.transpose(result, (1, 0, 2)).reshape(queries.shape[0], -1).astype(jnp.bfloat16)

def reference(video_in, text_in, mod_video, mod_text, qkv_video, qkv_text, proj_video, proj_text, gain_video, gain_text, windows, text_len):
    hblocks = N_SEQ // (FRAMES // TT)
    v_dev = TT * HT_DEV * TH * W
    normed_video = modulate(video_in, mod_video)
    normed_text = modulate(text_in, mod_text)
    proj_v = jnp.dot(normed_video, qkv_video.reshape(D, 3 * D), preferred_element_type=jnp.float32).reshape(-1, 3, D)
    proj_t = jnp.dot(normed_text, qkv_text.reshape(D, 3 * D), preferred_element_type=jnp.float32).reshape(-1, 3, D)
    query_v, key_v, value_v = finish_qkv(proj_v, gain_video)
    query_t, key_t, value_t = finish_qkv(proj_t, gain_text)
    text_ok = jnp.arange(TEXT, dtype=jnp.int32) < text_len[0]
    offsets = [t_off + h_off for t_off in (0, -hblocks, hblocks) for h_off in (0, -1, 1)]

    def one_block(block_index):
        query_pos = tile_coords(block_index, v_dev, hblocks)
        queries = lax.dynamic_slice_in_dim(query_v, block_index * v_dev, v_dev, 0).reshape(v_dev, HEADS, HD)
        key_list = []
        value_list = []
        mask_list = []
        for offset in offsets:
            source = block_index + offset
            present = (source >= 0) & (source < N_SEQ)
            clipped = jnp.clip(source, 0, N_SEQ - 1).astype(jnp.int32)
            key_pos = tile_coords(clipped, v_dev, hblocks)
            mask_list.append(window_mask(query_pos, key_pos, windows) & present)
            key_list.append(lax.dynamic_slice_in_dim(key_v, clipped * v_dev, v_dev, 0))
            value_list.append(lax.dynamic_slice_in_dim(value_v, clipped * v_dev, v_dev, 0))
        mask_list.append(jnp.broadcast_to(text_ok[None, None, :], (HEADS, v_dev, TEXT)))
        key_vecs = jnp.concatenate(key_list + [key_t], 0).reshape(-1, HEADS, HD)
        value_vecs = jnp.concatenate(value_list + [value_t], 0).reshape(-1, HEADS, HD)
        allowed = jnp.concatenate(mask_list, 2)
        return softmax_attend(queries, key_vecs, value_vecs, allowed)
    attended_v = lax.map(one_block, jnp.arange(N_SEQ, dtype=jnp.int32)).reshape(-1, D)
    video_total = key_v.shape[0]
    text_keys = jnp.concatenate([key_v, key_t], 0).reshape(-1, HEADS, HD)
    text_values = jnp.concatenate([value_v, value_t], 0).reshape(-1, HEADS, HD)
    text_allowed = jnp.concatenate([jnp.ones((HEADS, TEXT, video_total), bool), jnp.broadcast_to(text_ok[None, None, :], (HEADS, TEXT, TEXT))], 2)
    attended_t = softmax_attend(query_t.reshape(TEXT, HEADS, HD), text_keys, text_values, text_allowed)
    branch_video = jnp.dot(attended_v, proj_video, preferred_element_type=jnp.float32)
    branch_text = jnp.dot(attended_t, proj_text, preferred_element_type=jnp.float32)
    video_out = (video_in.astype(jnp.float32) + mod_video[2] * branch_video).astype(jnp.bfloat16)
    text_out = (text_in.astype(jnp.float32) + mod_text[2] * branch_text).astype(jnp.bfloat16)
    return (video_out, text_out)
```

```python
import math

import jax
import jax.numpy as jnp
from jax import lax
from jax.experimental import pallas as pl
from jax.experimental.pallas import tpu as pltpu
from jax.sharding import PartitionSpec as P

MESH = pl.DeviceIdType.MESH
BF = jnp.bfloat16
F32 = jnp.float32
ROWS = 640
WIDE = 1152
PART = 384
SHARD = 192
HD = 128
TILES = 5
NEG_BIG = -1e30
SCALE2 = math.log2(math.e) / math.sqrt(HD)

GATHER = ("PO", "Y", "L", "R", "LY", "RY", "Da", "Db", "DYa", "DYb",
          "PY", "PL", "PR", "PLY", "PRY", "PDa", "PDb", "PDYa", "PDYb")
GID = {k: i for i, k in enumerate(GATHER)}
RING = ("Up", "Dn", "H", "HUp", "HDn", "D2a", "D2b", "HD2a", "HD2b")
RID = {k: i for i, k in enumerate(RING)}


def remote(src, dst, send, recv, seq=None, head=None):
    to = {}
    if seq is not None:
        to["seq"] = seq
    if head is not None:
        to["head"] = head
    return pltpu.make_async_remote_copy(
        src_ref=src, dst_ref=dst, send_sem=send, recv_sem=recv,
        device_id=to, device_id_type=MESH)


def head_normed(vals, gain):
    return vals * lax.rsqrt(jnp.mean(jnp.square(vals), axis=1, keepdims=True) + 1e-6) * gain


def with_ones(value):
    return jnp.concatenate([value, jnp.ones_like(value)], axis=1)


def kernel(vid, txt, modv, modt, w, wt, pv, pt, gainv, gaint, windows, text_len,
           video_out, text_out,
           normed, wbuf, acc, nt, tnt, part, ppart, tsum_in, tall,
           q, kv, kvbuf, top, att, attbuf, wp, acc2,
           ts, ts_in, atg, tpart, tpart_in,
           own_sem, send, recv, tsend, trecv, rsend, rrecv, gsend, grecv,
           ksend, krecv, zsend, zrecv, wsend, wrecv, psend, precv,
           msend, mrecv, asend, arecv, osend, orecv):
    s = lax.axis_index("seq")
    h = lax.axis_index("head")
    y, x, c = s // 8, (s % 8) // 2, s % 2
    z, yh = h % 4, h // 4
    chip = y * 4 + x

    def seq_of(y, x, c):
        return y * 8 + x * 2 + c

    partner = seq_of(y, x, 1 - c)
    ynbr = seq_of(1 - y, x, c)
    xl, xr, xd = (x + 3) % 4, (x + 1) % 4, (x + 2) % 4
    left, right = seq_of(y, xl, c), seq_of(y, xr, c)
    xnbr = seq_of(y, (x + 3 + 2 * c) % 4, 1 - c)
    slots = {"O": chip, "Y": (1 - y) * 4 + x, "L": y * 4 + xl, "R": y * 4 + xr,
             "LY": (1 - y) * 4 + xl, "RY": (1 - y) * 4 + xr,
             "D": y * 4 + xd, "DY": (1 - y) * 4 + xd}
    up, dn, hn = yh * 4 + (z + 1) % 4, yh * 4 + (z + 3) % 4, (1 - yh) * 4 + z
    places = {"O": h, "Up": up, "Dn": dn, "H": hn,
              "HUp": (1 - yh) * 4 + (z + 1) % 4, "HDn": (1 - yh) * 4 + (z + 3) % 4,
              "D2": yh * 4 + (z + 2) % 4, "HD2": (1 - yh) * 4 + (z + 2) % 4}
    home = jnp.where(h == s // 2, 1, 0)

    barrier = pltpu.get_barrier_semaphore()

    def greet(d, carry):
        pl.semaphore_signal(barrier, inc=1, device_id={"seq": (s + d) % 16}, device_id_type=MESH)
        return carry

    lax.fori_loop(1, 16, greet, 0)
    for peer in (up, dn, hn):
        pl.semaphore_signal(barrier, inc=1, device_id={"head": peer}, device_id_type=MESH)

    def greet_far(i, carry):
        far_s, far_h = 2 * h + i % 2, i // 2

        @pl.when(jnp.logical_or(far_s != s, far_h != h))
        def _():
            pl.semaphore_signal(barrier, inc=1, device_id={"seq": far_s, "head": far_h},
                                device_id_type=MESH)
        return carry

    lax.fori_loop(0, 16, greet_far, 0)
    pl.semaphore_wait(barrier, 15 + 3 + 16 - home)

    sent = []

    class Gather:
        def __init__(self, buf, ssem, rsem, cut):
            self.buf, self.ssem, self.rsem, self.cut = buf, ssem, rsem, cut

        def view(self, place, core, half):
            ref = self.buf.at[slots[place], core]
            if half == "":
                return ref
            return ref.at[pl.ds(0 if half == "a" else self.cut, self.cut)]

        def push(self, place, core, half, kind, to, src=None):
            ref = self.view(place, core, half)
            cp = remote(ref if src is None else src, ref, self.ssem.at[GID[kind]],
                        self.rsem.at[GID[kind]], to)
            cp.start()
            sent.append(cp)

        def arrive(self, place, core, half, kind):
            ref = self.view(place, core, half)
            remote(ref, ref, self.ssem.at[GID[kind]], self.rsem.at[GID[kind]], partner).wait_recv()

    wg = Gather(wbuf, send, recv, SHARD // 2)
    pg = Gather(wp, psend, precv, 4)

    wg.push("O", c, "", "Y", ynbr, src=w)
    wg.push("O", c, "", "L", right, src=w)
    wg.push("O", c, "", "R", left, src=w)
    wg.push("O", c, "", "PO", partner, src=w)
    keep = pltpu.make_async_copy(w, wbuf.at[chip, c], own_sem.at[0])
    keep.start()

    def layer_norm(vals, shift, scale):
        vals = vals.astype(F32)
        vals = vals - jnp.mean(vals, axis=1, keepdims=True)
        spread = jnp.mean(jnp.square(vals), axis=1, keepdims=True)
        return (vals * lax.rsqrt(spread + 1e-6) * scale + shift).astype(BF)

    text_normed = layer_norm(txt[...], modt[pl.ds(0, 1), :], 1.0 + modt[pl.ds(1, 1), :])
    for d in range(16):
        nt[d] = text_normed[:, d * SHARD:(d + 1) * SHARD]
    own_row = c * 8 + chip

    def scatter(d, carry):
        to = (s + d) % 16
        remote(nt.at[to], tnt.at[own_row], tsend.at[d], trecv.at[d], to).start()
        return carry

    lax.fori_loop(1, 16, scatter, 0)
    keep_t = pltpu.make_async_copy(nt.at[s], tnt.at[own_row], own_sem.at[1])
    keep_t.start()

    def pieces(j, carry):
        to_s, to_h = 2 * j + c, s // 2
        here = jnp.logical_and(to_s == s, to_h == h)

        @pl.when(jnp.logical_not(here))
        def _():
            remote(pv.at[:, j], wp.at[j, c, h], wsend.at[j], wrecv.at[h], to_s, to_h).start()

        @pl.when(here)
        def _():
            pltpu.make_async_copy(pv.at[:, j], wp.at[j, c, h], own_sem.at[2]).start()
        return carry

    lax.fori_loop(0, 8, pieces, 0)

    shift = modv[pl.ds(0, 1), :]
    scale = 1.0 + modv[pl.ds(1, 1), :]

    def norm_rows(i, carry):
        to = (i % TILES) * 8 + i // TILES
        normed[pl.ds(pl.multiple_of(to * 16, 16), 16), :] = layer_norm(
            vid[pl.ds(pl.multiple_of(i * 16, 16), 16), :], shift, scale)
        return carry

    lax.fori_loop(0, 40, norm_rows, 0)

    def scattered(d, carry):
        remote(nt.at[0], tnt.at[0], tsend.at[d], trecv.at[d], partner).wait_recv()
        return carry

    lax.fori_loop(1, 16, scattered, 0)
    keep_t.wait()
    for g in range(3):
        cols = pl.ds(g * PART, PART)
        part[:, :, :, cols] = jnp.dot(
            tnt[...].reshape(256, SHARD), wt[:, cols], preferred_element_type=F32
        ).reshape(2, 8, 16, PART)
    swap = remote(part.at[1 - c], ppart, rsend.at[0], rrecv.at[0], partner)
    swap.start()

    wg.arrive("L", c, "", "L")
    wg.push("L", c, "a", "Da", right)
    wg.arrive("R", c, "", "R")
    wg.push("R", c, "b", "Db", left)
    wg.arrive("Y", c, "", "Y")
    wg.push("Y", c, "", "RY", left)
    wg.push("Y", c, "", "LY", right)
    wg.push("L", c, "", "PL", partner)
    wg.push("R", c, "", "PR", partner)
    wg.push("Y", c, "", "PY", partner)

    swap.wait()
    part[pl.ds(c, 1)] = part[pl.ds(c, 1)] + ppart[...].reshape(1, 8, 16, WIDE)

    def reduce_send(d, carry):
        j = (chip + d) % 8
        remote(part.at[c, j], tsum_in.at[d], rsend.at[d], rrecv.at[d], 2 * j + c).start()
        return carry

    lax.fori_loop(1, 8, reduce_send, 0)

    def multiply(place, first=False):
        j = slots[place]
        lhs = normed[:, pl.ds(pl.multiple_of(j * PART, PART), PART)]
        for g in range(3):
            cols = pl.ds(g * PART, PART)
            term = jnp.dot(lhs, wbuf[j, :, :, cols].reshape(PART, PART), preferred_element_type=F32)
            if first:
                acc[:, cols] = term
            else:
                acc[:, cols] += term

    keep.wait()
    wg.arrive("O", 1 - c, "", "PO")
    multiply("O", True)
    wg.arrive("Y", 1 - c, "", "PY")
    multiply("Y")
    wg.arrive("L", 1 - c, "", "PL")
    multiply("L")
    wg.arrive("D", c, "a", "Da")
    wg.push("D", c, "a", "DYa", ynbr)
    wg.push("D", c, "a", "PDa", partner)
    wg.arrive("D", c, "b", "Db")
    wg.push("D", c, "b", "DYb", ynbr)
    wg.push("D", c, "b", "PDb", partner)
    wg.arrive("R", 1 - c, "", "PR")
    multiply("R")
    wg.arrive("LY", c, "", "LY")
    wg.push("LY", c, "", "PLY", partner)
    wg.arrive("RY", c, "", "RY")
    wg.push("RY", c, "", "PRY", partner)
    wg.arrive("D", 1 - c, "a", "PDa")
    wg.arrive("D", 1 - c, "b", "PDb")
    multiply("D")
    wg.arrive("DY", c, "a", "DYa")
    wg.push("DY", c, "a", "PDYa", partner)
    wg.arrive("LY", 1 - c, "", "PLY")
    multiply("LY")
    wg.arrive("DY", c, "b", "DYb")
    wg.push("DY", c, "b", "PDYb", partner)
    wg.arrive("RY", 1 - c, "", "PRY")
    multiply("RY")
    wg.arrive("DY", 1 - c, "a", "PDYa")
    wg.arrive("DY", 1 - c, "b", "PDYb")
    multiply("DY")

    def kv_push(k, n, to, src=None):
        src = kv.at[n] if src is None else src
        cp = remote(src, kvbuf.at[k, n], ksend.at[k, n], krecv.at[k, n], to)
        cp.start()
        sent.append(cp)

    def kv_arrive(k, n):
        ref = kvbuf.at[k, n]
        remote(ref, ref, ksend.at[k, n], krecv.at[k, n], partner).wait_recv()

    for n in range(3):
        def finish(i, carry, n=n):
            rows = pl.ds(pl.multiple_of(i * 128, 128), 128)
            kv[n, rows, :HD] = head_normed(
                acc[rows, PART + n * HD:PART + (n + 1) * HD], gainv[pl.ds(1, 1), :]).astype(BF)
            kv[n, rows, HD:] = acc[rows, 2 * PART + n * HD:2 * PART + (n + 1) * HD].astype(BF)
            return carry

        lax.fori_loop(0, TILES, finish, 0)
        kv_push(1, n, ynbr)
        if n < 2:
            kv_push(3, n, xnbr)
        kv_push(0, n, partner)

    def finish_q(i, carry):
        rows = pl.ds(pl.multiple_of(i * 128, 128), 128)
        for n in range(3):
            q[n, rows] = head_normed(acc[rows, n * HD:(n + 1) * HD], gainv[pl.ds(0, 1), :]).astype(BF)
        return carry

    lax.fori_loop(0, TILES, finish_q, 0)

    def reduced(d, carry):
        remote(part.at[0, 0], tsum_in.at[d], rsend.at[d], rrecv.at[d], partner).wait_recv()
        return carry

    lax.fori_loop(1, 8, reduced, 0)
    total = part[pl.ds(c, 1), pl.ds(chip, 1)].reshape(16, WIDE)
    for d in range(1, 8):
        total = total + tsum_in[d]
    for n in range(6):
        hd = total[:, n * HD:(n + 1) * HD]
        tall[pl.ds(s, 1), :, n * HD:(n + 1) * HD] = head_normed(
            hd, gaint[pl.ds(n // 3, 1), :]).astype(BF).reshape(1, 16, HD)
    tall[pl.ds(s, 1), :, 768:] = total[:, 768:].astype(BF).reshape(1, 16, PART)

    def give(d, carry):
        j = (chip + d) % 8
        remote(tall.at[s], tall.at[s], gsend.at[d], grecv.at[d], 2 * j + c).start()
        return carry

    lax.fori_loop(1, 8, give, 0)
    remote(tall.at[s], tall.at[s], gsend.at[0], grecv.at[0], partner).start()

    height = 2 * x + c
    x_there = jnp.where(jnp.logical_or(jnp.logical_and(height == 0, c == 0),
                                       jnp.logical_and(height == 7, c == 1)), 0, 1)
    lane_tile = lax.broadcasted_iota(jnp.int32, (1, ROWS), 1) // 128

    def attend(n, keys, values, bias_of, first=False):
        def tile(i, carry):
            rows = pl.ds(pl.multiple_of(i * 128, 128), 128)
            t = lax.dot_general(q[n, rows], keys(), (((1,), (1,)), ((), ())),
                                preferred_element_type=F32) * SCALE2 + bias_of(i)
            peak = jnp.max(t, axis=1, keepdims=True)
            if first:
                new = peak
            else:
                old = top[n, rows, :]
                new = jnp.maximum(old, peak)
            p = jnp.exp2(t - new[:, :1]).astype(BF)
            gain = jnp.dot(p, with_ones(values()), preferred_element_type=F32)
            if first:
                att[n, rows, :] = gain
            else:
                factor = jnp.exp2(old - new)
                att[n, rows, :] = att[n, rows, :] * jnp.concatenate([factor, factor], axis=1) + gain
            top[n, rows, :] = jnp.broadcast_to(new, (128, HD))
            return carry

        lax.fori_loop(0, TILES, tile, 0)

    def window_bias(n, dt, dh, there):
        row = h * 3 + n
        fits = jnp.logical_and(windows[row, 0] >= dt, windows[row, 1] >= dh)
        reach = jnp.where(fits, windows[row, 2], -1)
        if there is not None:
            reach = jnp.where(there == 1, reach, -1)
        return lambda i: jnp.where(jnp.abs(lane_tile - i) <= reach, 0.0, NEG_BIG)

    def attend_block(k, n):
        dt = 1 if k in (1, 2, 4) else 0
        dh = 1 if k in (0, 2, 3, 4) else 0
        there = x_there if k in (3, 4) else None
        attend(n, lambda: kvbuf[k, n, :, :HD], lambda: kvbuf[k, n, :, HD:], window_bias(n, dt, dh, there))

    for n in range(3):
        attend(n, lambda n=n: kv[n, :, :HD], lambda n=n: kv[n, :, HD:], window_bias(n, 0, 0, None), True)

    for d in range(1, 8):
        j = (chip + 8 - d) % 8
        block = tall.at[2 * j + c]
        remote(block, block, gsend.at[d], grecv.at[d], partner).wait_recv()
        remote(block, block, gsend.at[7 + d], grecv.at[7 + d], partner).start()
    for n in range(3):
        kv_arrive(0, n)
        attend_block(0, n)
    for d in range(1, 8):
        j = (chip + 8 - d) % 8
        block = tall.at[2 * j + 1 - c]
        remote(block, block, gsend.at[7 + d], grecv.at[7 + d], partner).wait_recv()
    block = tall.at[partner]
    remote(block, block, gsend.at[0], grecv.at[0], partner).wait_recv()

    def text_cols(g, n):
        return tall[:, :, g * PART + n * HD:g * PART + (n + 1) * HD].reshape(256, HD)

    lane = lax.broadcasted_iota(jnp.int32, (16, HD), 1)

    def text_part(i, carry):
        blocks = pl.ds(i * 8, 8)
        stat = jnp.zeros((128, HD), F32)
        lanes = lax.broadcasted_iota(jnp.int32, (128, HD), 1)
        for n in range(3):
            tq = tall[blocks, :, n * HD:(n + 1) * HD].reshape(128, HD)
            t = lax.dot_general(tq, kv[n, :, :HD], (((1,), (1,)), ((), ())),
                                preferred_element_type=F32) * SCALE2
            peak = jnp.max(t, axis=1, keepdims=True)
            p = jnp.exp2(t - peak).astype(BF)
            both = jnp.dot(p, with_ones(kv[n, :, HD:]), preferred_element_type=F32)
            ts[blocks, :, n * HD:(n + 1) * HD] = (both[:, :HD] / both[:, HD:]).reshape(8, 16, HD)
            stat = jnp.where(lanes == n, peak + jnp.log2(both[:, HD:]), stat)
        ts[blocks, :, PART:] = stat.reshape(8, 16, HD)
        return carry

    lax.fori_loop(0, 2, text_part, 0)

    def merge_send(d, carry):
        to = (s + d) % 16
        remote(ts.at[to], ts_in.at[d], msend.at[d], mrecv.at[d], to).start()
        return carry

    lax.fori_loop(1, 16, merge_send, 0)

    text_row = jnp.where(lax.broadcasted_iota(jnp.int32, (1, 256), 1) < text_len[0], 0.0, NEG_BIG)

    def attend_text(n):
        attend(n, lambda: text_cols(1, n), lambda: text_cols(2, n), lambda i: text_row)

    def ring_push(place, n, half, kind, to):
        ref = attbuf.at[places[place], n]
        if half:
            ref = ref.at[pl.ds(0 if half == "a" else ROWS // 2, ROWS // 2)]
        cp = remote(ref, ref, zsend.at[RID[kind], n], zrecv.at[RID[kind], n], None, to)
        cp.start()
        sent.append(cp)

    def ring_arrive(place, n, half, kind):
        ref = attbuf.at[places[place], n]
        if half:
            ref = ref.at[pl.ds(0 if half == "a" else ROWS // 2, ROWS // 2)]
        remote(ref, ref, zsend.at[RID[kind], n], zrecv.at[RID[kind], n], None, up).wait_recv()

    def close_head(n):
        def tile(i, carry):
            rows = pl.ds(pl.multiple_of(i * 128, 128), 128)
            attbuf[pl.ds(h, 1), n, rows, :] = (
                att[n, rows, :HD] / att[n, rows, HD:]).astype(BF).reshape(1, 128, HD)
            return carry

        lax.fori_loop(0, TILES, tile, 0)
        ring_push("O", n, "", "H", hn)
        ring_push("O", n, "", "Dn", up)
        ring_push("O", n, "", "Up", dn)

    def ring_one(n):
        ring_arrive("H", n, "", "H")
        ring_push("H", n, "", "HDn", up)
        ring_push("H", n, "", "HUp", dn)
        ring_arrive("Dn", n, "", "Dn")
        ring_push("Dn", n, "a", "D2a", up)
        ring_arrive("Up", n, "", "Up")
        ring_push("Up", n, "b", "D2b", dn)

    def ring_two(n):
        ring_arrive("HDn", n, "", "HDn")
        ring_push("HDn", n, "a", "HD2a", up)
        ring_arrive("HUp", n, "", "HUp")
        ring_push("HUp", n, "b", "HD2b", dn)

    def ring_three(n):
        for half in ("a", "b"):
            ring_arrive("D2", n, half, "D2" + half)
            ring_arrive("HD2", n, half, "HD2" + half)

    def project(n, first=False):
        def one(j, carry):
            rhs = jnp.concatenate(
                [wp[:, 0, j, n].reshape(HD, SHARD), wp[:, 1, j, n].reshape(HD, SHARD)], axis=1)
            acc2[...] += jnp.dot(attbuf[j, n], rhs, preferred_element_type=F32)
            return carry

        lax.fori_loop(0, 8, one, 0)

    kv_arrive(1, 0)
    kv_push(4, 0, xnbr, kvbuf.at[1, 0])
    kv_push(3, 2, xnbr)
    kv_push(2, 0, partner, kvbuf.at[1, 0])
    attend_text(0)
    attend_block(1, 0)
    kv_arrive(2, 0)
    attend_block(2, 0)
    kv_arrive(3, 0)
    attend_block(3, 0)
    attend_text(1)
    attend_text(2)
    kv_arrive(4, 0)
    attend_block(4, 0)
    close_head(0)

    kv_arrive(1, 1)
    kv_push(4, 1, xnbr, kvbuf.at[1, 1])
    kv_push(2, 1, partner, kvbuf.at[1, 1])
    attend_block(1, 1)
    kv_arrive(2, 1)
    attend_block(2, 1)
    kv_arrive(3, 1)
    attend_block(3, 1)
    ring_one(0)

    def piece(j, carry):
        @pl.when(jnp.logical_not(jnp.logical_and(s // 2 == h, j == h)))
        def _():
            remote(wp.at[0, 0, 0], wp.at[chip, c, j], wsend.at[0], wrecv.at[j], partner).wait_recv()
        return carry

    lax.fori_loop(0, 8, piece, 0)

    @pl.when(home == 1)
    def _():
        pltpu.make_async_copy(pv.at[:, 0], wp.at[chip, c, h], own_sem.at[2]).wait()

    pg.push("O", c, "", "Y", ynbr)
    pg.push("O", c, "", "L", right)
    pg.push("O", c, "", "R", left)
    pg.push("O", c, "", "PO", partner)

    kv_arrive(4, 1)
    attend_block(4, 1)
    close_head(1)
    ring_two(0)

    kv_arrive(1, 2)
    kv_push(4, 2, xnbr, kvbuf.at[1, 2])
    kv_push(2, 2, partner, kvbuf.at[1, 2])
    attend_block(1, 2)
    kv_arrive(2, 2)
    attend_block(2, 2)
    kv_arrive(3, 2)
    attend_block(3, 2)
    ring_one(1)

    def merge_wait(d, carry):
        remote(ts.at[0], ts_in.at[d], msend.at[d], mrecv.at[d], partner).wait_recv()
        return carry

    lax.fori_loop(1, 16, merge_wait, 0)
    ts_in[0] = ts[pl.ds(s, 1)].reshape(16, 512)
    for n in range(3):
        tq = tall[pl.ds(s, 1), :, n * HD:(n + 1) * HD].reshape(16, HD)
        t = lax.dot_general(tq, text_cols(1, n), (((1,), (1,)), ((), ())),
                            preferred_element_type=F32) * SCALE2 + text_row
        peak = jnp.max(t, axis=1, keepdims=True)
        p = jnp.exp2(t - peak).astype(BF)
        both = jnp.dot(p, with_ones(text_cols(2, n)), preferred_element_type=F32)
        logs = [ts_in[d, :, PART + n:PART + n + 1] for d in range(16)]
        high = peak + jnp.log2(both[:, HD:HD + 1])
        for value in logs:
            high = jnp.maximum(high, value)
        weight = jnp.exp2(peak - high)
        upper = both[:, :HD] * weight
        lower = both[:, HD:HD + 1] * weight
        for d in range(16):
            weight = jnp.exp2(logs[d] - high)
            upper = upper + ts_in[d, :, n * HD:(n + 1) * HD] * weight
            lower = lower + weight
        atg[pl.ds(s, 1), :, n * HD:(n + 1) * HD] = (upper / lower).astype(BF).reshape(1, 16, HD)

    def text_give(d, carry):
        remote(atg.at[s], atg.at[s], asend.at[d], arecv.at[d], (s + d) % 16).start()
        return carry

    lax.fori_loop(1, 16, text_give, 0)

    pg.arrive("L", c, "", "L")
    pg.push("L", c, "a", "Da", right)
    pg.arrive("R", c, "", "R")
    pg.push("R", c, "b", "Db", left)
    pg.arrive("Y", c, "", "Y")
    pg.push("Y", c, "", "RY", left)
    pg.push("Y", c, "", "LY", right)
    pg.push("L", c, "", "PL", partner)
    pg.push("R", c, "", "PR", partner)
    pg.push("Y", c, "", "PY", partner)

    kv_arrive(4, 2)
    attend_block(4, 2)
    close_head(2)
    ring_two(1)

    pg.arrive("D", c, "a", "Da")
    pg.push("D", c, "a", "DYa", ynbr)
    pg.push("D", c, "a", "PDa", partner)
    pg.arrive("D", c, "b", "Db")
    pg.push("D", c, "b", "DYb", ynbr)
    pg.push("D", c, "b", "PDb", partner)
    pg.arrive("LY", c, "", "LY")
    pg.push("LY", c, "", "PLY", partner)
    pg.arrive("RY", c, "", "RY")
    pg.push("RY", c, "", "PRY", partner)

    def text_given(d, carry):
        block = atg.at[(s + 16 - d) % 16]
        remote(block, block, asend.at[d], arecv.at[d], partner).wait_recv()
        return carry

    lax.fori_loop(1, 16, text_given, 0)
    tpart[...] = jnp.dot(atg[...].reshape(256, PART), pt[...],
                         preferred_element_type=F32).reshape(16, 16, SHARD)

    def text_move(i, carry):
        here = jnp.logical_and(i == s, s // 2 == h)

        @pl.when(jnp.logical_not(here))
        def _():
            remote(tpart.at[i], tpart_in.at[c, h], osend.at[i], orecv.at[c, h], i, s // 2).start()

        @pl.when(here)
        def _():
            pltpu.make_async_copy(tpart.at[i], tpart_in.at[c, h], own_sem.at[3]).start()
        return carry

    lax.fori_loop(0, 16, text_move, 0)

    ring_one(2)
    pg.arrive("DY", c, "a", "DYa")
    pg.push("DY", c, "a", "PDYa", partner)
    pg.arrive("DY", c, "b", "DYb")
    pg.push("DY", c, "b", "PDYb", partner)
    pg.arrive("O", 1 - c, "", "PO")
    for place in ("Y", "L", "R", "LY", "RY"):
        pg.arrive(place, 1 - c, "", "P" + place)
    for half in ("a", "b"):
        pg.arrive("D", 1 - c, half, "PD" + half)
        pg.arrive("DY", 1 - c, half, "PDY" + half)
    acc2[...] = jnp.zeros_like(acc2)
    ring_three(0)
    project(0)
    ring_two(2)
    ring_three(1)
    project(1)

    def text_moved(i, carry):
        @pl.when(jnp.logical_not(jnp.logical_and(2 * h + i % 2 == s, i // 2 == h)))
        def _():
            remote(tpart.at[0], tpart_in.at[i % 2, i // 2], osend.at[0], orecv.at[i % 2, i // 2],
                   partner).wait_recv()
        return carry

    lax.fori_loop(0, 16, text_moved, 0)

    @pl.when(home == 1)
    def _():
        pltpu.make_async_copy(tpart.at[0], tpart_in.at[c, h], own_sem.at[3]).wait()

    out_cols = pl.ds(pl.multiple_of(h * PART, PART), PART)
    sums = jnp.concatenate([jnp.sum(tpart_in[0], axis=0), jnp.sum(tpart_in[1], axis=0)], axis=1)
    text_out[...] = (txt[:, out_cols].astype(F32) + modt[pl.ds(2, 1), out_cols] * sums).astype(BF)

    ring_three(2)
    project(2)
    gate = modv[pl.ds(2, 1), out_cols]

    def write(i, carry):
        rows = pl.ds(pl.multiple_of(i * 16, 16), 16)
        at = pl.ds(pl.multiple_of(((i % TILES) * 8 + i // TILES) * 16, 16), 16)
        video_out[rows, :] = (vid[rows, out_cols].astype(F32) + gate * acc2[at, :]).astype(BF)
        return carry

    lax.fori_loop(0, 40, write, 0)

    def left_t(d, carry):
        remote(nt.at[0], tnt.at[0], tsend.at[d], trecv.at[d], partner).wait_send()
        remote(ts.at[0], ts_in.at[0], msend.at[d], mrecv.at[d], partner).wait_send()
        remote(atg.at[0], atg.at[0], asend.at[d], arecv.at[d], partner).wait_send()
        return carry

    lax.fori_loop(1, 16, left_t, 0)

    def left_r(d, carry):
        remote(part.at[0, 0], tsum_in.at[d], rsend.at[d], rrecv.at[d], partner).wait_send()
        return carry

    lax.fori_loop(1, 8, left_r, 0)

    def left_g(d, carry):
        remote(tall.at[0], tall.at[0], gsend.at[d], grecv.at[d], partner).wait_send()
        return carry

    lax.fori_loop(0, 15, left_g, 0)

    def left_w(j, carry):
        @pl.when(jnp.logical_not(jnp.logical_and(2 * j + c == s, s // 2 == h)))
        def _():
            remote(pv.at[:, 0], wp.at[0, 0, 0], wsend.at[j], wrecv.at[0], partner).wait_send()
        return carry

    lax.fori_loop(0, 8, left_w, 0)

    def left_o(i, carry):
        @pl.when(jnp.logical_not(jnp.logical_and(i == s, s // 2 == h)))
        def _():
            remote(tpart.at[0], tpart_in.at[0, 0], osend.at[i], orecv.at[0, 0], partner).wait_send()
        return carry

    lax.fori_loop(0, 16, left_o, 0)
    for cp in sent:
        cp.wait_send()


def block_kernel(vid, txt, modv, modt, w, wt, pv, pt, gainv, gaint, windows, text_len):
    vm = pl.BlockSpec(memory_space=pltpu.VMEM)
    sm = pl.BlockSpec(memory_space=pltpu.SMEM)
    dma = pltpu.SemaphoreType.DMA
    v = pltpu.VMEM
    return pl.pallas_call(
        kernel,
        name="attention_block",
        out_shape=(jax.ShapeDtypeStruct((ROWS, PART), BF), jax.ShapeDtypeStruct((16, PART), BF)),
        in_specs=[vm] * 10 + [sm, sm],
        out_specs=(vm, vm),
        scratch_shapes=[
            v((ROWS, 3072), BF), v((8, 2, SHARD, WIDE), BF), v((ROWS, WIDE), F32),
            v((16, 16, SHARD), BF), v((16, 16, SHARD), BF),
            v((2, 8, 16, WIDE), F32), v((8, 16, WIDE), F32), v((8, 16, WIDE), F32),
            v((16, 16, WIDE), BF),
            v((3, ROWS, HD), BF), v((3, ROWS, 2 * HD), BF), v((5, 3, ROWS, 2 * HD), BF),
            v((3, ROWS, HD), F32), v((3, ROWS, 2 * HD), F32), v((8, 3, ROWS, HD), BF),
            v((8, 2, 8, 3, 16, SHARD), BF), v((ROWS, PART), F32),
            v((16, 16, 512), F32), v((16, 16, 512), F32), v((16, 16, PART), BF),
            v((16, 16, SHARD), F32), v((2, 8, 16, SHARD), F32),
            dma((4,)), dma((19,)), dma((19,)), dma((16,)), dma((16,)),
            dma((8,)), dma((8,)), dma((15,)), dma((15,)),
            dma((5, 3)), dma((5, 3)), dma((9, 3)), dma((9, 3)),
            dma((8,)), dma((8,)), dma((19,)), dma((19,)),
            dma((16,)), dma((16,)), dma((16,)), dma((16,)), dma((16,)), dma((2, 8)),
        ],
        compiler_params=pltpu.CompilerParams(
            collective_id=1, has_side_effects=True, vmem_limit_bytes=58 * 2**20),
    )(vid, txt, modv, modt, w, wt, pv, pt, gainv, gaint, windows, text_len)


def body(video_in, text_in, mod_video, mod_text, qkv_video, qkv_text, proj_video, proj_text,
         gain_video, gain_text, windows, text_len):
    return block_kernel(
        video_in, text_in, mod_video, mod_text,
        qkv_video.reshape(SHARD, WIDE), qkv_text.reshape(SHARD, WIDE),
        proj_video.reshape(3, 8, 16, SHARD), proj_text,
        gain_video, gain_text, windows, text_len)


def solution(mesh):
    return jax.shard_map(
        body,
        mesh=mesh,
        in_specs=(
            P("seq", None), P("seq", None), P(), P(),
            P("seq", None, "head"), P("seq", None, "head"),
            P("head", "seq"), P("head", "seq"), P(), P(), P(), P(),
        ),
        out_specs=(P("seq", "head"), P("seq", "head")),
        check_vma=False,
    )
```

```python
import math

import jax
import jax.numpy as jnp
from jax import lax
from jax.experimental import pallas as pl
from jax.experimental.pallas import tpu as pltpu
from jax.sharding import PartitionSpec as P

MESH = pl.DeviceIdType.MESH
BF = jnp.bfloat16
F32 = jnp.float32
ROWS = 640
WIDE = 1152
PART = 384
SHARD = 192
HD = 128
TILES = 5
NEG_BIG = -1e30
SCALE2 = math.log2(math.e) / math.sqrt(HD)

GATHER = ("PO", "Y", "L", "R", "LY", "RY", "Da", "Db", "DYa", "DYb",
          "PY", "PL", "PR", "PLY", "PRY", "PDa", "PDb", "PDYa", "PDYb")
GID = {k: i for i, k in enumerate(GATHER)}
RING = ("Up", "Dn", "H", "HUp", "HDn", "D2a", "D2b", "HD2a", "HD2b")
RID = {k: i for i, k in enumerate(RING)}


def remote(src, dst, send, recv, seq=None, head=None):
    to = {}
    if seq is not None:
        to["seq"] = seq
    if head is not None:
        to["head"] = head
    return pltpu.make_async_remote_copy(
        src_ref=src, dst_ref=dst, send_sem=send, recv_sem=recv,
        device_id=to, device_id_type=MESH)


def head_normed(vals, gain):
    return vals * lax.rsqrt(jnp.mean(jnp.square(vals), axis=1, keepdims=True) + 1e-6) * gain


def with_ones(value):
    return jnp.concatenate([value, jnp.ones_like(value)], axis=1)


def kernel(vid_hbm, txt, modv, modt, w, wt_hbm, pv_hbm, pt_hbm, gainv, gaint, windows, text_len,
           video_out, text_out,
           vid, wt, pvt, pt, pv, normed, wbuf, acc, nt, tnt, part, ppart, tsum_in, tall,
           q, kv, kvbuf, top, att, attbuf, wp, acc2,
           ts, ts_in, atg, tpart, tpart_in,
           own_sem, send, recv, tsend, trecv, rsend, rrecv, gsend, grecv,
           ksend, krecv, zsend, zrecv, wsend, wrecv, psend, precv,
           msend, mrecv, asend, arecv, osend, orecv):
    s = lax.axis_index("seq")
    h = lax.axis_index("head")
    y, x, c = s // 8, (s % 8) // 2, s % 2
    z, yh = h % 4, h // 4
    chip = y * 4 + x

    def seq_of(y, x, c):
        return y * 8 + x * 2 + c

    partner = seq_of(y, x, 1 - c)
    ynbr = seq_of(1 - y, x, c)
    xl, xr, xd = (x + 3) % 4, (x + 1) % 4, (x + 2) % 4
    left, right = seq_of(y, xl, c), seq_of(y, xr, c)
    xnbr = seq_of(y, (x + 3 + 2 * c) % 4, 1 - c)
    slots = {"O": chip, "Y": (1 - y) * 4 + x, "L": y * 4 + xl, "R": y * 4 + xr,
             "LY": (1 - y) * 4 + xl, "RY": (1 - y) * 4 + xr,
             "D": y * 4 + xd, "DY": (1 - y) * 4 + xd}
    up, dn, hn = yh * 4 + (z + 1) % 4, yh * 4 + (z + 3) % 4, (1 - yh) * 4 + z
    places = {"O": h, "Up": up, "Dn": dn, "H": hn,
              "HUp": (1 - yh) * 4 + (z + 1) % 4, "HDn": (1 - yh) * 4 + (z + 3) % 4,
              "D2": yh * 4 + (z + 2) % 4, "HD2": (1 - yh) * 4 + (z + 2) % 4}
    home = jnp.where(h == s // 2, 1, 0)

    def fetch(i, src, dst):
        cp = pltpu.make_async_copy(src, dst, own_sem.at[i])
        cp.start()
        return cp

    def shard(n):
        return w.at[:, :, pl.ds(n * HD, HD)]

    fetch_vid = fetch(4, vid_hbm, vid)
    fetch_pv = fetch(5, pv_hbm, pvt)
    fetch_wt = fetch(6, wt_hbm, wt)
    fetch_pt = fetch(7, pt_hbm, pt)
    keep = [fetch(8 + n, shard(n), wbuf.at[n, chip, c]) for n in range(3)]

    barrier = pltpu.get_barrier_semaphore()

    def greet(d, carry):
        pl.semaphore_signal(barrier, inc=1, device_id={"seq": (s + d) % 16}, device_id_type=MESH)
        return carry

    lax.fori_loop(1, 16, greet, 0)
    for peer in (up, dn, hn):
        pl.semaphore_signal(barrier, inc=1, device_id={"head": peer}, device_id_type=MESH)

    def greet_far(i, carry):
        far_s, far_h = 2 * h + i % 2, i // 2

        @pl.when(jnp.logical_or(far_s != s, far_h != h))
        def _():
            pl.semaphore_signal(barrier, inc=1, device_id={"seq": far_s, "head": far_h},
                                device_id_type=MESH)
        return carry

    lax.fori_loop(0, 16, greet_far, 0)
    pl.semaphore_wait(barrier, 15 + 3 + 16 - home)

    sent = []

    class Gather:
        def __init__(self, at, ssem, rsem, cut):
            self.at, self.ssem, self.rsem, self.cut = at, ssem, rsem, cut

        def view(self, place, core, half):
            ref = self.at(slots[place], core)
            return self.cut(ref, half) if half else ref

        def push(self, place, core, half, kind, to, src=None):
            ref = self.view(place, core, half)
            cp = remote(ref if src is None else src, ref, self.ssem.at[GID[kind]],
                        self.rsem.at[GID[kind]], to)
            cp.start()
            sent.append(cp)

        def arrive(self, place, core, half, kind):
            ref = self.view(place, core, half)
            remote(ref, ref, self.ssem.at[GID[kind]], self.rsem.at[GID[kind]], partner).wait_recv()

        def own(self, src=None):
            self.push("O", c, "", "L", right, src)
            self.push("O", c, "", "R", left, src)
            self.push("O", c, "", "Y", ynbr, src)
            self.push("O", c, "", "PO", partner, src)

        def one(self):
            self.arrive("L", c, "", "L")
            self.push("L", c, "a", "Da", right)
            self.arrive("R", c, "", "R")
            self.push("R", c, "b", "Db", left)
            self.arrive("Y", c, "", "Y")
            self.push("Y", c, "", "RY", left)
            self.push("Y", c, "", "LY", right)
            self.push("L", c, "", "PL", partner)
            self.push("R", c, "", "PR", partner)
            self.push("Y", c, "", "PY", partner)

        def two(self):
            for half in ("a", "b"):
                self.arrive("D", c, half, "D" + half)
                self.push("D", c, half, "DY" + half, ynbr)
                self.push("D", c, half, "PD" + half, partner)
            for place in ("LY", "RY"):
                self.arrive(place, c, "", place)
                self.push(place, c, "", "P" + place, partner)

        def three(self):
            for half in ("a", "b"):
                self.arrive("DY", c, half, "DY" + half)
                self.push("DY", c, half, "PDY" + half, partner)

        def pair(self, place):
            if place in ("D", "DY"):
                for half in ("a", "b"):
                    self.arrive(place, 1 - c, half, "P" + place + half)
            else:
                self.arrive(place, 1 - c, "", "P" + place)

    def cut_weights(ref, half):
        return ref.at[:, pl.ds(0 if half == "a" else SHARD // 2, SHARD // 2)]

    def cut_pieces(ref, half):
        return ref.at[pl.ds(0 if half == "a" else 4, 4)]

    wg = [Gather(lambda j, core, n=n: wbuf.at[n, j, core], send.at[n], recv.at[n], cut_weights)
          for n in range(3)]
    pg = Gather(lambda j, core: wp.at[j, core], psend, precv, cut_pieces)

    wg[0].own(shard(0))
    wg[1].own(shard(1))

    def layer_norm(vals, shift, scale):
        vals = vals.astype(F32)
        vals = vals - jnp.mean(vals, axis=1, keepdims=True)
        spread = jnp.mean(jnp.square(vals), axis=1, keepdims=True)
        return (vals * lax.rsqrt(spread + 1e-6) * scale + shift).astype(BF)

    text_normed = layer_norm(txt[...], modt[pl.ds(0, 1), :], 1.0 + modt[pl.ds(1, 1), :])
    for d in range(16):
        nt[d] = text_normed[:, d * SHARD:(d + 1) * SHARD]
    own_row = c * 8 + chip

    def scatter(d, carry):
        to = (s + d) % 16
        remote(nt.at[to], tnt.at[own_row], tsend.at[d], trecv.at[d], to).start()
        return carry

    lax.fori_loop(1, 16, scatter, 0)
    keep_t = pltpu.make_async_copy(nt.at[s], tnt.at[own_row], own_sem.at[1])
    keep_t.start()

    shift = modv[pl.ds(0, 1), :]
    scale = 1.0 + modv[pl.ds(1, 1), :]

    def norm_rows(i, carry):
        to = (i % TILES) * 8 + i // TILES
        normed[pl.ds(pl.multiple_of(to * 16, 16), 16), :] = layer_norm(
            vid[pl.ds(pl.multiple_of(i * 16, 16), 16), :], shift, scale)
        return carry

    fetch_vid.wait()
    lax.fori_loop(0, 40, norm_rows, 0, unroll=4)
    wg[0].one()

    def scattered(d, carry):
        remote(nt.at[0], tnt.at[0], tsend.at[d], trecv.at[d], partner).wait_recv()
        return carry

    lax.fori_loop(1, 16, scattered, 0)
    keep_t.wait()
    fetch_wt.wait()
    for g in range(3):
        part[:, :, :, g * PART:(g + 1) * PART] = jnp.dot(
            tnt[...].reshape(256, SHARD), wt[g], preferred_element_type=F32
        ).reshape(2, 8, 16, PART)
    swap = remote(part.at[1 - c], ppart, rsend.at[0], rrecv.at[0], partner)
    swap.start()
    wg[2].own(shard(2))
    fetch_pv.wait()
    pv[...] = pvt[...].astype(F32).T.astype(BF).reshape(3, 8, 16, SHARD)

    def pieces(j, carry):
        to_s, to_h = 2 * j + c, s // 2
        here = jnp.logical_and(to_s == s, to_h == h)

        @pl.when(jnp.logical_not(here))
        def _():
            remote(pv.at[:, j], wp.at[j, c, h], wsend.at[j], wrecv.at[h], to_s, to_h).start()

        @pl.when(here)
        def _():
            pltpu.make_async_copy(pv.at[:, j], wp.at[j, c, h], own_sem.at[2]).start()
        return carry

    lax.fori_loop(0, 8, pieces, 0)

    def multiply(n, place, first=False):
        wg[n].pair(place)
        j = slots[place]
        lhs = normed[:, pl.ds(pl.multiple_of(j * PART, PART), PART)]
        rhs = jnp.concatenate([wbuf[n, j, :, g].reshape(PART, HD) for g in range(3)], axis=1)
        term = jnp.dot(lhs, rhs, preferred_element_type=F32)
        if first:
            acc[n] = term
        else:
            acc[n] += term

    keep[0].wait()
    multiply(0, "O", True)
    wg[1].one()
    multiply(0, "Y")
    multiply(0, "L")
    multiply(0, "R")
    wg[0].two()
    swap.wait()
    part[pl.ds(c, 1)] = part[pl.ds(c, 1)] + ppart[...].reshape(1, 8, 16, WIDE)

    def reduce_send(d, carry):
        j = (chip + d) % 8
        remote(part.at[c, j], tsum_in.at[d], rsend.at[d], rrecv.at[d], 2 * j + c).start()
        return carry

    lax.fori_loop(1, 8, reduce_send, 0)

    keep[1].wait()
    multiply(1, "O", True)
    wg[2].one()
    multiply(0, "LY")
    multiply(0, "RY")
    multiply(0, "D")
    multiply(1, "Y")
    multiply(1, "L")
    multiply(1, "R")
    wg[1].two()
    wg[0].three()
    multiply(0, "DY")

    def kv_push(k, n, to, src=None):
        src = kv.at[n] if src is None else src
        cp = remote(src, kvbuf.at[k, n], ksend.at[k, n], krecv.at[k, n], to)
        cp.start()
        sent.append(cp)

    def kv_arrive(k, n):
        ref = kvbuf.at[k, n]
        remote(ref, ref, ksend.at[k, n], krecv.at[k, n], partner).wait_recv()

    def finish(n):
        def keys(i, carry):
            rows = pl.ds(i * 128, 128)
            kv[n, rows, :HD] = head_normed(acc[n, rows, HD:2 * HD], gainv[pl.ds(1, 1), :]).astype(BF)
            kv[n, rows, HD:] = acc[n, rows, 2 * HD:].astype(BF)
            return carry

        def queries(i, carry):
            rows = pl.ds(i * 128, 128)
            q[n, rows] = head_normed(acc[n, rows, :HD], gainv[pl.ds(0, 1), :]).astype(BF)
            return carry

        lax.fori_loop(0, TILES, keys, 0, unroll=True)
        kv_push(1, n, ynbr)
        kv_push(3, n, xnbr)
        kv_push(0, n, partner)
        lax.fori_loop(0, TILES, queries, 0, unroll=True)

    def kv_forward(n):
        kv_arrive(1, n)
        kv_push(4, n, xnbr, kvbuf.at[1, n])
        kv_push(2, n, partner, kvbuf.at[1, n])

    height = 2 * x + c
    x_there = jnp.where(jnp.logical_or(jnp.logical_and(height == 0, c == 0),
                                       jnp.logical_and(height == 7, c == 1)), 0, 1)
    lane_tile = lax.broadcasted_iota(jnp.int32, (1, ROWS), 1) // 128

    def attend(n, keys, values, bias_of, first=False):
        def tile(i, carry):
            rows = pl.ds(pl.multiple_of(i * 128, 128), 128)
            t = lax.dot_general(q[n, rows], keys(), (((1,), (1,)), ((), ())),
                                preferred_element_type=F32) * SCALE2 + bias_of(i)
            peak = jnp.max(t, axis=1, keepdims=True)
            if first:
                new = peak
            else:
                old = top[n, rows, :]
                new = jnp.maximum(old, peak)
            p = jnp.exp2(t - new[:, :1]).astype(BF)
            gain = jnp.dot(p, with_ones(values()), preferred_element_type=F32)
            if first:
                att[n, rows, :] = gain
            else:
                factor = jnp.exp2(old - new)
                att[n, rows, :] = att[n, rows, :] * jnp.concatenate([factor, factor], axis=1) + gain
            top[n, rows, :] = jnp.broadcast_to(new, (128, HD))
            return carry

        lax.fori_loop(0, TILES, tile, 0, unroll=True)

    def window_bias(n, dt, dh, there):
        row = h * 3 + n
        fits = jnp.logical_and(windows[0, row] >= dt, windows[1, row] >= dh)
        reach = jnp.where(fits, windows[2, row], -1)
        if there is not None:
            reach = jnp.where(there == 1, reach, -1)
        return lambda i: jnp.where(jnp.abs(lane_tile - i) <= reach, 0.0, NEG_BIG)

    def attend_block(k, n):
        dt = 1 if k in (1, 2, 4) else 0
        dh = 1 if k in (0, 2, 3, 4) else 0
        there = x_there if k in (3, 4) else None
        attend(n, lambda: kvbuf[k, n, :, :HD], lambda: kvbuf[k, n, :, HD:], window_bias(n, dt, dh, there))

    def text_cols(g, n):
        return tall[:, :, g * PART + n * HD:g * PART + (n + 1) * HD].reshape(256, HD)

    lane = lax.broadcasted_iota(jnp.int32, (16, HD), 1)

    def text_part(i, carry):
        blocks = pl.ds(i * 8, 8)
        stat = jnp.zeros((128, HD), F32)
        lanes = lax.broadcasted_iota(jnp.int32, (128, HD), 1)
        for n in range(3):
            tq = tall[blocks, :, n * HD:(n + 1) * HD].reshape(128, HD)
            t = lax.dot_general(tq, kv[n, :, :HD], (((1,), (1,)), ((), ())),
                                preferred_element_type=F32) * SCALE2
            peak = jnp.max(t, axis=1, keepdims=True)
            p = jnp.exp2(t - peak).astype(BF)
            both = jnp.dot(p, with_ones(kv[n, :, HD:]), preferred_element_type=F32)
            ts[blocks, :, n * HD:(n + 1) * HD] = (both[:, :HD] / both[:, HD:]).reshape(8, 16, HD)
            stat = jnp.where(lanes == n, peak + jnp.log2(both[:, HD:]), stat)
        ts[blocks, :, PART:] = stat.reshape(8, 16, HD)
        return carry

    text_row = jnp.where(lax.broadcasted_iota(jnp.int32, (1, 256), 1) < text_len[0], 0.0, NEG_BIG)

    def attend_text(n):
        attend(n, lambda: text_cols(1, n), lambda: text_cols(2, n), lambda i: text_row)

    def ring_push(place, n, half, kind, to):
        ref = attbuf.at[places[place], n]
        if half:
            ref = ref.at[pl.ds(0 if half == "a" else ROWS // 2, ROWS // 2)]
        cp = remote(ref, ref, zsend.at[RID[kind], n], zrecv.at[RID[kind], n], None, to)
        cp.start()
        sent.append(cp)

    def ring_arrive(place, n, half, kind):
        ref = attbuf.at[places[place], n]
        if half:
            ref = ref.at[pl.ds(0 if half == "a" else ROWS // 2, ROWS // 2)]
        remote(ref, ref, zsend.at[RID[kind], n], zrecv.at[RID[kind], n], None, up).wait_recv()

    def close_head(n):
        def tile(i, carry):
            rows = pl.ds(pl.multiple_of(i * 128, 128), 128)
            attbuf[pl.ds(h, 1), n, rows, :] = (
                att[n, rows, :HD] / att[n, rows, HD:]).astype(BF).reshape(1, 128, HD)
            return carry

        lax.fori_loop(0, TILES, tile, 0, unroll=True)
        ring_push("O", n, "", "H", hn)
        ring_push("O", n, "", "Dn", up)
        ring_push("O", n, "", "Up", dn)

    def ring_one(n):
        ring_arrive("Dn", n, "", "Dn")
        ring_push("Dn", n, "a", "D2a", up)
        ring_arrive("Up", n, "", "Up")
        ring_push("Up", n, "b", "D2b", dn)
        ring_arrive("H", n, "", "H")
        ring_push("H", n, "", "HDn", up)
        ring_push("H", n, "", "HUp", dn)

    def ring_two(n):
        for half in ("a", "b"):
            ring_arrive("D2", n, half, "D2" + half)
            ring_push("D2", n, half, "HD2" + half, hn)

    def ring_three(n):
        ring_arrive("HDn", n, "", "HDn")
        ring_arrive("HUp", n, "", "HUp")
        for half in ("a", "b"):
            ring_arrive("HD2", n, half, "HD2" + half)

    def project(n, first=False):
        for j in range(0, 8, 2):
            rhs = jnp.concatenate(
                [jnp.concatenate([wp[:, core, j + e, n].reshape(HD, SHARD) for core in range(2)], axis=1)
                 for e in range(2)], axis=0)
            lhs = jnp.concatenate([attbuf[j, n], attbuf[j + 1, n]], axis=1)
            term = jnp.dot(lhs, rhs, preferred_element_type=F32)
            if first and j == 0:
                acc2[...] = term
            else:
                acc2[...] += term

    def attend_own(n):
        attend(n, lambda: kv[n, :, :HD], lambda: kv[n, :, HD:], window_bias(n, 0, 0, None), True)

    def attend_other(k, n):
        if k != 1:
            kv_arrive(k, n)
        attend_block(k, n)

    finish(0)
    attend_own(0)
    multiply(1, "LY")
    multiply(1, "RY")
    multiply(1, "D")
    keep[2].wait()
    multiply(2, "O", True)
    multiply(2, "Y")
    multiply(2, "L")
    multiply(2, "R")
    wg[2].two()
    wg[1].three()
    multiply(1, "DY")
    finish(1)
    kv_forward(0)

    def reduced(d, carry):
        remote(part.at[0, 0], tsum_in.at[d], rsend.at[d], rrecv.at[d], partner).wait_recv()
        return carry

    lax.fori_loop(1, 8, reduced, 0)
    total = part[pl.ds(c, 1), pl.ds(chip, 1)].reshape(16, WIDE)
    for d in range(1, 8):
        total = total + tsum_in[d]
    for n in range(6):
        hd = total[:, n * HD:(n + 1) * HD]
        tall[pl.ds(s, 1), :, n * HD:(n + 1) * HD] = head_normed(
            hd, gaint[pl.ds(n // 3, 1), :]).astype(BF).reshape(1, 16, HD)
    tall[pl.ds(s, 1), :, 768:] = total[:, 768:].astype(BF).reshape(1, 16, PART)

    def give(d, carry):
        j = (chip + d) % 8
        remote(tall.at[s], tall.at[s], gsend.at[d], grecv.at[d], 2 * j + c).start()
        return carry

    lax.fori_loop(1, 8, give, 0)
    remote(tall.at[s], tall.at[s], gsend.at[0], grecv.at[0], partner).start()

    attend_own(1)
    attend_other(0, 0)
    attend_other(1, 0)
    multiply(2, "LY")
    multiply(2, "RY")
    multiply(2, "D")
    wg[2].three()
    multiply(2, "DY")
    finish(2)

    for d in range(1, 8):
        j = (chip + 8 - d) % 8
        block = tall.at[2 * j + c]
        remote(block, block, gsend.at[d], grecv.at[d], partner).wait_recv()
        remote(block, block, gsend.at[7 + d], grecv.at[7 + d], partner).start()
    attend_own(2)
    attend_other(0, 1)
    attend_other(2, 0)
    attend_other(3, 0)
    kv_forward(1)
    attend_other(1, 1)
    for d in range(1, 8):
        j = (chip + 8 - d) % 8
        block = tall.at[2 * j + 1 - c]
        remote(block, block, gsend.at[7 + d], grecv.at[7 + d], partner).wait_recv()
    block = tall.at[partner]
    remote(block, block, gsend.at[0], grecv.at[0], partner).wait_recv()
    lax.fori_loop(0, 2, text_part, 0, unroll=True)

    def merge_send(d, carry):
        to = (s + d) % 16
        remote(ts.at[to], ts_in.at[d], msend.at[d], mrecv.at[d], to).start()
        return carry

    lax.fori_loop(1, 16, merge_send, 0)
    attend_text(0)
    attend_other(4, 0)
    close_head(0)
    attend_text(1)
    attend_text(2)

    def piece(j, carry):
        @pl.when(jnp.logical_not(jnp.logical_and(s // 2 == h, j == h)))
        def _():
            remote(wp.at[0, 0, 0], wp.at[chip, c, j], wsend.at[0], wrecv.at[j], partner).wait_recv()
        return carry

    lax.fori_loop(0, 8, piece, 0)

    @pl.when(home == 1)
    def _():
        pltpu.make_async_copy(pv.at[:, 0], wp.at[chip, c, h], own_sem.at[2]).wait()

    attend_other(0, 2)
    attend_other(2, 1)
    attend_other(3, 1)
    kv_forward(2)
    pg.own()
    attend_other(1, 2)
    attend_other(4, 1)
    close_head(1)
    ring_one(0)
    attend_other(2, 2)
    attend_other(3, 2)
    pg.one()

    def merge_wait(d, carry):
        remote(ts.at[0], ts_in.at[d], msend.at[d], mrecv.at[d], partner).wait_recv()
        return carry

    lax.fori_loop(1, 16, merge_wait, 0)
    ts_in[0] = ts[pl.ds(s, 1)].reshape(16, 512)
    for n in range(3):
        tq = tall[pl.ds(s, 1), :, n * HD:(n + 1) * HD].reshape(16, HD)
        t = lax.dot_general(tq, text_cols(1, n), (((1,), (1,)), ((), ())),
                            preferred_element_type=F32) * SCALE2 + text_row
        peak = jnp.max(t, axis=1, keepdims=True)
        p = jnp.exp2(t - peak).astype(BF)
        both = jnp.dot(p, with_ones(text_cols(2, n)), preferred_element_type=F32)
        logs = [ts_in[d, :, PART + n:PART + n + 1] for d in range(16)]
        high = peak + jnp.log2(both[:, HD:HD + 1])
        for value in logs:
            high = jnp.maximum(high, value)
        weight = jnp.exp2(peak - high)
        upper = both[:, :HD] * weight
        lower = both[:, HD:HD + 1] * weight
        for d in range(16):
            weight = jnp.exp2(logs[d] - high)
            upper = upper + ts_in[d, :, n * HD:(n + 1) * HD] * weight
            lower = lower + weight
        atg[pl.ds(s, 1), :, n * HD:(n + 1) * HD] = (upper / lower).astype(BF).reshape(1, 16, HD)

    def text_give(d, carry):
        remote(atg.at[s], atg.at[s], asend.at[d], arecv.at[d], (s + d) % 16).start()
        return carry

    lax.fori_loop(1, 16, text_give, 0)

    attend_other(4, 2)
    close_head(2)
    ring_two(0)
    ring_one(1)
    pg.two()

    fetch_pt.wait()
    def text_given(d, carry):
        block = atg.at[(s + 16 - d) % 16]
        remote(block, block, asend.at[d], arecv.at[d], partner).wait_recv()
        return carry

    lax.fori_loop(1, 16, text_given, 0)
    tpart[...] = lax.dot_general(
        atg[...].reshape(256, PART), pt[...], (((1,), (1,)), ((), ())),
        preferred_element_type=F32).reshape(16, 16, SHARD)

    def text_move(i, carry):
        here = jnp.logical_and(i == s, s // 2 == h)

        @pl.when(jnp.logical_not(here))
        def _():
            remote(tpart.at[i], tpart_in.at[c, h], osend.at[i], orecv.at[c, h], i, s // 2).start()

        @pl.when(here)
        def _():
            pltpu.make_async_copy(tpart.at[i], tpart_in.at[c, h], own_sem.at[3]).start()
        return carry

    lax.fori_loop(0, 16, text_move, 0)

    ring_one(2)
    ring_two(1)
    pg.three()
    for place in ("O", "Y", "L", "R", "LY", "RY", "D", "DY"):
        pg.pair(place)
    ring_three(0)
    project(0, True)
    ring_two(2)
    ring_three(1)
    project(1)

    def text_moved(i, carry):
        @pl.when(jnp.logical_not(jnp.logical_and(2 * h + i % 2 == s, i // 2 == h)))
        def _():
            remote(tpart.at[0], tpart_in.at[i % 2, i // 2], osend.at[0], orecv.at[i % 2, i // 2],
                   partner).wait_recv()
        return carry

    lax.fori_loop(0, 16, text_moved, 0)

    @pl.when(home == 1)
    def _():
        pltpu.make_async_copy(tpart.at[0], tpart_in.at[c, h], own_sem.at[3]).wait()

    out_cols = pl.ds(pl.multiple_of(h * PART, PART), PART)
    sums = jnp.concatenate([jnp.sum(tpart_in[0], axis=0), jnp.sum(tpart_in[1], axis=0)], axis=1)
    text_out[...] = (txt[:, out_cols].astype(F32) + modt[pl.ds(2, 1), out_cols] * sums).astype(BF)

    ring_three(2)
    project(2)
    gate = modv[pl.ds(2, 1), out_cols]

    def write(i, carry):
        rows = pl.ds(pl.multiple_of(i * 16, 16), 16)
        at = pl.ds(pl.multiple_of(((i % TILES) * 8 + i // TILES) * 16, 16), 16)
        video_out[rows, :] = (vid[rows, out_cols].astype(F32) + gate * acc2[at, :]).astype(BF)
        return carry

    lax.fori_loop(0, 40, write, 0, unroll=4)

    def left_t(d, carry):
        remote(nt.at[0], tnt.at[0], tsend.at[d], trecv.at[d], partner).wait_send()
        remote(ts.at[0], ts_in.at[0], msend.at[d], mrecv.at[d], partner).wait_send()
        remote(atg.at[0], atg.at[0], asend.at[d], arecv.at[d], partner).wait_send()
        return carry

    lax.fori_loop(1, 16, left_t, 0)

    def left_r(d, carry):
        remote(part.at[0, 0], tsum_in.at[d], rsend.at[d], rrecv.at[d], partner).wait_send()
        return carry

    lax.fori_loop(1, 8, left_r, 0)

    def left_g(d, carry):
        remote(tall.at[0], tall.at[0], gsend.at[d], grecv.at[d], partner).wait_send()
        return carry

    lax.fori_loop(0, 15, left_g, 0)

    def left_w(j, carry):
        @pl.when(jnp.logical_not(jnp.logical_and(2 * j + c == s, s // 2 == h)))
        def _():
            remote(pv.at[:, 0], wp.at[0, 0, 0], wsend.at[j], wrecv.at[0], partner).wait_send()
        return carry

    lax.fori_loop(0, 8, left_w, 0)

    def left_o(i, carry):
        @pl.when(jnp.logical_not(jnp.logical_and(i == s, s // 2 == h)))
        def _():
            remote(tpart.at[0], tpart_in.at[0, 0], osend.at[i], orecv.at[0, 0], partner).wait_send()
        return carry

    lax.fori_loop(0, 16, left_o, 0)
    for cp in sent:
        cp.wait_send()


def block_kernel(vid, txt, modv, modt, w, wt, pv, pt, gainv, gaint, windows, text_len):
    vm = pl.BlockSpec(memory_space=pltpu.VMEM)
    sm = pl.BlockSpec(memory_space=pltpu.SMEM)
    hbm = pl.BlockSpec(memory_space=pl.ANY)
    dma = pltpu.SemaphoreType.DMA
    v = pltpu.VMEM
    return pl.pallas_call(
        kernel,
        name="attention_block",
        out_shape=(jax.ShapeDtypeStruct((ROWS, PART), BF), jax.ShapeDtypeStruct((16, PART), BF)),
        in_specs=[hbm] + [vm] * 3 + [hbm] * 4 + [vm] * 2 + [sm, sm],
        out_specs=(vm, vm),
        scratch_shapes=[
            v((ROWS, 3072), BF), v((3, SHARD, PART), BF), v((SHARD, PART), BF), v((SHARD, PART), BF),
            v((3, 8, 16, SHARD), BF),
            v((ROWS, 3072), BF), v((3, 8, 2, 3, SHARD, HD), BF), v((3, ROWS, PART), F32),
            v((16, 16, SHARD), BF), v((16, 16, SHARD), BF),
            v((2, 8, 16, WIDE), F32), v((8, 16, WIDE), F32), v((8, 16, WIDE), F32),
            v((16, 16, WIDE), BF),
            v((3, ROWS, HD), BF), v((3, ROWS, 2 * HD), BF), v((5, 3, ROWS, 2 * HD), BF),
            v((3, ROWS, HD), F32), v((3, ROWS, 2 * HD), F32), v((8, 3, ROWS, HD), BF),
            v((8, 2, 8, 3, 16, SHARD), BF), v((ROWS, PART), F32),
            v((16, 16, 512), F32), v((16, 16, 512), F32), v((16, 16, PART), BF),
            v((16, 16, SHARD), F32), v((2, 8, 16, SHARD), F32),
            dma((11,)), dma((3, 19)), dma((3, 19)), dma((16,)), dma((16,)),
            dma((8,)), dma((8,)), dma((15,)), dma((15,)),
            dma((5, 3)), dma((5, 3)), dma((9, 3)), dma((9, 3)),
            dma((8,)), dma((8,)), dma((19,)), dma((19,)),
            dma((16,)), dma((16,)), dma((16,)), dma((16,)), dma((16,)), dma((2, 8)),
        ],
        compiler_params=pltpu.CompilerParams(
            collective_id=1, has_side_effects=True, vmem_limit_bytes=58 * 2**20),
    )(vid, txt, modv, modt, w, wt, pv, pt, gainv, gaint, windows, text_len)


def body(video_in, text_in, mod_video, mod_text, qkv_video, qkv_text, proj_video, proj_text,
         gain_video, gain_text, windows, text_len):
    return block_kernel(
        video_in, text_in, mod_video, mod_text,
        jnp.transpose(qkv_video, (1, 0, 2)), jnp.transpose(qkv_text, (1, 0, 2)),
        proj_video.T, proj_text.T,
        gain_video, gain_text, windows.T, text_len)


def solution(mesh):
    return jax.shard_map(
        body,
        mesh=mesh,
        in_specs=(
            P("seq", None), P("seq", None), P(), P(),
            P("seq", None, "head"), P("seq", None, "head"),
            P("head", "seq"), P("head", "seq"), P(), P(), P(), P(),
        ),
        out_specs=(P("seq", "head"), P("seq", "head")),
        check_vma=False,
    )
```

```python
import math

import jax
import jax.numpy as jnp
from jax import lax
from jax.experimental import pallas as pl
from jax.experimental.pallas import tpu as pltpu
from jax.sharding import PartitionSpec as P

MESH = pl.DeviceIdType.MESH
BF = jnp.bfloat16
F32 = jnp.float32
ROWS = 640
WIDE = 1152
PART = 384
SHARD = 192
HD = 128
TILES = 5
NEG_BIG = -1e30
SCALE2 = math.log2(math.e) / math.sqrt(HD)

GATHER = ("PO", "Y", "L", "R", "LY", "RY", "Da", "Db", "DYa", "DYb",
          "PY", "PL", "PR", "PLY", "PRY", "PDa", "PDb", "PDYa", "PDYb")
GID = {k: i for i, k in enumerate(GATHER)}
RING = ("Up", "Dn", "H", "HUp", "HDn", "D2a", "D2b", "HD2a", "HD2b")
RID = {k: i for i, k in enumerate(RING)}


def remote(src, dst, send, recv, seq=None, head=None):
    to = {}
    if seq is not None:
        to["seq"] = seq
    if head is not None:
        to["head"] = head
    return pltpu.make_async_remote_copy(
        src_ref=src, dst_ref=dst, send_sem=send, recv_sem=recv,
        device_id=to, device_id_type=MESH)


def head_normed(vals, gain):
    return vals * lax.rsqrt(jnp.mean(jnp.square(vals), axis=1, keepdims=True) + 1e-6) * gain


def with_ones(value):
    return jnp.concatenate([value, jnp.ones_like(value)], axis=1)


def kernel(vid_hbm, txt, modv, modt, w, wt_hbm, pv_hbm, pt_hbm, gainv, gaint, windows, text_len,
           video_out, text_out,
           vid, wt, pvt, pt, pv, normed, wbuf, acc, nt, tnt, part, ppart, tsum_in, tall,
           q, kv, kvbuf, top, att, attbuf, wp, acc2,
           ts, ts_in, atg, tpart, tpart_in,
           own_sem, send, recv, tsend, trecv, rsend, rrecv, gsend, grecv,
           ksend, krecv, zsend, zrecv, wsend, wrecv, psend, precv,
           msend, mrecv, asend, arecv, osend, orecv):
    s = lax.axis_index("seq")
    h = lax.axis_index("head")
    y, x, c = s // 8, (s % 8) // 2, s % 2
    z, yh = h % 4, h // 4
    chip = y * 4 + x

    def seq_of(y, x, c):
        return y * 8 + x * 2 + c

    partner = seq_of(y, x, 1 - c)
    ynbr = seq_of(1 - y, x, c)
    xl, xr, xd = (x + 3) % 4, (x + 1) % 4, (x + 2) % 4
    left, right = seq_of(y, xl, c), seq_of(y, xr, c)
    xnbr = seq_of(y, (x + 3 + 2 * c) % 4, 1 - c)
    slots = {"O": chip, "Y": (1 - y) * 4 + x, "L": y * 4 + xl, "R": y * 4 + xr,
             "LY": (1 - y) * 4 + xl, "RY": (1 - y) * 4 + xr,
             "D": y * 4 + xd, "DY": (1 - y) * 4 + xd}
    up, dn, hn = yh * 4 + (z + 1) % 4, yh * 4 + (z + 3) % 4, (1 - yh) * 4 + z
    places = {"O": h, "Up": up, "Dn": dn, "H": hn,
              "HUp": (1 - yh) * 4 + (z + 1) % 4, "HDn": (1 - yh) * 4 + (z + 3) % 4,
              "D2": yh * 4 + (z + 2) % 4, "HD2": (1 - yh) * 4 + (z + 2) % 4}
    home = jnp.where(h == s // 2, 1, 0)

    def fetch(i, src, dst):
        cp = pltpu.make_async_copy(src, dst, own_sem.at[i])
        cp.start()
        return cp

    def shard(n):
        return w.at[:, :, pl.ds(n * HD, HD)]

    fetch_vid = fetch(4, vid_hbm, vid)
    fetch_pv = fetch(5, pv_hbm, pvt)
    fetch_wt = fetch(6, wt_hbm, wt)
    fetch_pt = fetch(7, pt_hbm, pt)
    keep = [fetch(8 + n, shard(n), wbuf.at[n, chip, c]) for n in range(3)]

    barrier = pltpu.get_barrier_semaphore()

    def greet(d, carry):
        pl.semaphore_signal(barrier, inc=1, device_id={"seq": (s + d) % 16}, device_id_type=MESH)
        return carry

    lax.fori_loop(1, 16, greet, 0)
    for peer in (up, dn, hn):
        pl.semaphore_signal(barrier, inc=1, device_id={"head": peer}, device_id_type=MESH)

    def greet_far(i, carry):
        far_s, far_h = 2 * h + i % 2, i // 2

        @pl.when(jnp.logical_or(far_s != s, far_h != h))
        def _():
            pl.semaphore_signal(barrier, inc=1, device_id={"seq": far_s, "head": far_h},
                                device_id_type=MESH)
        return carry

    lax.fori_loop(0, 16, greet_far, 0)
    def layer_norm(vals, shift, scale):
        vals = vals.astype(F32)
        vals = vals - jnp.mean(vals, axis=1, keepdims=True)
        spread = jnp.mean(jnp.square(vals), axis=1, keepdims=True)
        return (vals * lax.rsqrt(spread + 1e-6) * scale + shift).astype(BF)

    text_normed = layer_norm(txt[...], modt[pl.ds(0, 1), :], 1.0 + modt[pl.ds(1, 1), :])
    for d in range(16):
        nt[d] = text_normed[:, d * SHARD:(d + 1) * SHARD]
    pl.semaphore_wait(barrier, 15 + 3 + 16 - home)

    sent = []

    class Gather:
        def __init__(self, at, ssem, rsem, cut):
            self.at, self.ssem, self.rsem, self.cut = at, ssem, rsem, cut

        def view(self, place, core, half):
            ref = self.at(slots[place], core)
            return self.cut(ref, half) if half else ref

        def push(self, place, core, half, kind, to, src=None):
            ref = self.view(place, core, half)
            cp = remote(ref if src is None else src, ref, self.ssem.at[GID[kind]],
                        self.rsem.at[GID[kind]], to)
            cp.start()
            sent.append(cp)

        def arrive(self, place, core, half, kind):
            ref = self.view(place, core, half)
            remote(ref, ref, self.ssem.at[GID[kind]], self.rsem.at[GID[kind]], partner).wait_recv()

        def own(self, src=None):
            self.push("O", c, "", "L", right, src)
            self.push("O", c, "", "R", left, src)
            self.push("O", c, "", "Y", ynbr, src)
            self.push("O", c, "", "PO", partner, src)

        def one(self):
            self.arrive("L", c, "", "L")
            self.push("L", c, "a", "Da", right)
            self.arrive("R", c, "", "R")
            self.push("R", c, "b", "Db", left)
            self.arrive("Y", c, "", "Y")
            self.push("Y", c, "", "RY", left)
            self.push("Y", c, "", "LY", right)
            self.push("L", c, "", "PL", partner)
            self.push("R", c, "", "PR", partner)
            self.push("Y", c, "", "PY", partner)

        def two(self):
            for half in ("a", "b"):
                self.arrive("D", c, half, "D" + half)
                self.push("D", c, half, "DY" + half, ynbr)
                self.push("D", c, half, "PD" + half, partner)
            for place in ("LY", "RY"):
                self.arrive(place, c, "", place)
                self.push(place, c, "", "P" + place, partner)

        def three(self):
            for half in ("a", "b"):
                self.arrive("DY", c, half, "DY" + half)
                self.push("DY", c, half, "PDY" + half, partner)

        def pair(self, place):
            if place in ("D", "DY"):
                for half in ("a", "b"):
                    self.arrive(place, 1 - c, half, "P" + place + half)
            else:
                self.arrive(place, 1 - c, "", "P" + place)

    def cut_weights(ref, half):
        return ref.at[:, pl.ds(0 if half == "a" else SHARD // 2, SHARD // 2)]

    def cut_pieces(ref, half):
        return ref.at[pl.ds(0 if half == "a" else 4, 4)]

    wg = [Gather(lambda j, core, n=n: wbuf.at[n, j, core], send.at[n], recv.at[n], cut_weights)
          for n in range(3)]
    pg = Gather(lambda j, core: wp.at[j, core], psend, precv, cut_pieces)

    wg[0].own(shard(0))

    own_row = c * 8 + chip

    def scatter(d, carry):
        to = (s + d) % 16
        remote(nt.at[to], tnt.at[own_row], tsend.at[d], trecv.at[d], to).start()
        return carry

    lax.fori_loop(1, 16, scatter, 0)
    keep_t = pltpu.make_async_copy(nt.at[s], tnt.at[own_row], own_sem.at[1])
    keep_t.start()
    wg[1].own(shard(1))

    shift = modv[pl.ds(0, 1), :]
    scale = 1.0 + modv[pl.ds(1, 1), :]

    def norm_rows(i, carry):
        to = (i % TILES) * 8 + i // TILES
        normed[pl.ds(pl.multiple_of(to * 16, 16), 16), :] = layer_norm(
            vid[pl.ds(pl.multiple_of(i * 16, 16), 16), :], shift, scale)
        return carry

    fetch_vid.wait()
    lax.fori_loop(0, 40, norm_rows, 0, unroll=4)
    wg[0].one()

    def scattered(d, carry):
        remote(nt.at[0], tnt.at[0], tsend.at[d], trecv.at[d], partner).wait_recv()
        return carry

    lax.fori_loop(1, 16, scattered, 0)
    keep_t.wait()
    fetch_wt.wait()
    for g in range(3):
        part[:, :, :, g * PART:(g + 1) * PART] = jnp.dot(
            tnt[...].reshape(256, SHARD), wt[g], preferred_element_type=F32
        ).reshape(2, 8, 16, PART)
    swap = remote(part.at[1 - c], ppart, rsend.at[0], rrecv.at[0], partner)
    swap.start()
    wg[2].own(shard(2))
    fetch_pv.wait()
    pv[...] = pvt[...].astype(F32).T.astype(BF).reshape(3, 8, 16, SHARD)

    def pieces(j, carry):
        to_s, to_h = 2 * j + c, s // 2
        here = jnp.logical_and(to_s == s, to_h == h)

        @pl.when(jnp.logical_not(here))
        def _():
            remote(pv.at[:, j], wp.at[j, c, h], wsend.at[j], wrecv.at[h], to_s, to_h).start()

        @pl.when(here)
        def _():
            pltpu.make_async_copy(pv.at[:, j], wp.at[j, c, h], own_sem.at[2]).start()
        return carry

    lax.fori_loop(0, 8, pieces, 0)

    def multiply(n, place, first=False):
        wg[n].pair(place)
        j = slots[place]
        lhs = normed[:, pl.ds(pl.multiple_of(j * PART, PART), PART)]
        rhs = jnp.concatenate([wbuf[n, j, :, g].reshape(PART, HD) for g in range(3)], axis=1)
        term = jnp.dot(lhs, rhs, preferred_element_type=F32)
        if first:
            acc[n] = term
        else:
            acc[n] += term

    keep[0].wait()
    multiply(0, "O", True)
    swap.wait()
    part[pl.ds(c, 1)] = part[pl.ds(c, 1)] + ppart[...].reshape(1, 8, 16, WIDE)

    across = remote(part.at[c, pl.ds((1 - y) * 4, 4)], tsum_in.at[pl.ds(0, 4)],
                    rsend.at[1], rrecv.at[1], ynbr)
    across.start()
    wg[1].one()
    multiply(0, "Y")
    multiply(0, "L")
    multiply(0, "R")
    wg[0].two()
    keep[1].wait()
    multiply(1, "O", True)
    wg[2].one()
    multiply(0, "LY")
    multiply(0, "RY")
    multiply(0, "D")
    multiply(1, "Y")
    multiply(1, "L")
    multiply(1, "R")
    wg[1].two()
    wg[0].three()
    multiply(0, "DY")
    def kv_push(k, n, to, src=None):
        src = kv.at[n] if src is None else src
        cp = remote(src, kvbuf.at[k, n], ksend.at[k, n], krecv.at[k, n], to)
        cp.start()
        sent.append(cp)

    def kv_arrive(k, n):
        ref = kvbuf.at[k, n]
        remote(ref, ref, ksend.at[k, n], krecv.at[k, n], partner).wait_recv()

    def finish(n):
        def keys(i, carry):
            rows = pl.ds(i * 128, 128)
            kv[n, rows, :HD] = head_normed(acc[n, rows, HD:2 * HD], gainv[pl.ds(1, 1), :]).astype(BF)
            kv[n, rows, HD:] = acc[n, rows, 2 * HD:].astype(BF)
            return carry

        def queries(i, carry):
            rows = pl.ds(i * 128, 128)
            q[n, rows] = head_normed(acc[n, rows, :HD], gainv[pl.ds(0, 1), :]).astype(BF)
            return carry

        lax.fori_loop(0, TILES, keys, 0, unroll=True)
        kv_push(1, n, ynbr)
        kv_push(3, n, xnbr)
        kv_push(0, n, partner)
        lax.fori_loop(0, TILES, queries, 0, unroll=True)

    def kv_forward(n):
        kv_arrive(1, n)
        kv_push(4, n, xnbr, kvbuf.at[1, n])
        kv_push(2, n, partner, kvbuf.at[1, n])

    height = 2 * x + c
    x_there = jnp.where(jnp.logical_or(jnp.logical_and(height == 0, c == 0),
                                       jnp.logical_and(height == 7, c == 1)), 0, 1)
    lane_tile = lax.broadcasted_iota(jnp.int32, (1, ROWS), 1) // 128

    def attend(n, keys, values, bias_of, first=False, tiles=(0, TILES)):
        def tile(i, carry):
            rows = pl.ds(pl.multiple_of(i * 128, 128), 128)
            t = lax.dot_general(q[n, rows], keys(), (((1,), (1,)), ((), ())),
                                preferred_element_type=F32) * SCALE2 + bias_of(i)
            peak = jnp.max(t, axis=1, keepdims=True)
            if first:
                new = peak
            else:
                old = top[n, rows, :]
                new = jnp.maximum(old, peak)
            p = jnp.exp2(t - new[:, :1]).astype(BF)
            gain = jnp.dot(p, with_ones(values()), preferred_element_type=F32)
            if first:
                att[n, rows, :] = gain
            else:
                factor = jnp.exp2(old - new)
                att[n, rows, :] = att[n, rows, :] * jnp.concatenate([factor, factor], axis=1) + gain
            top[n, rows, :] = jnp.broadcast_to(new, (128, HD))
            return carry

        lax.fori_loop(*tiles, tile, 0, unroll=True)

    def window_bias(n, dt, dh, there):
        row = h * 3 + n
        fits = jnp.logical_and(windows[0, row] >= dt, windows[1, row] >= dh)
        reach = jnp.where(fits, windows[2, row], -1)
        if there is not None:
            reach = jnp.where(there == 1, reach, -1)
        return lambda i: jnp.where(jnp.abs(lane_tile - i) <= reach, 0.0, NEG_BIG)

    def attend_block(k, n, tiles=(0, TILES)):
        dt = 1 if k in (1, 2, 4) else 0
        dh = 1 if k in (0, 2, 3, 4) else 0
        there = x_there if k in (3, 4) else None
        attend(n, lambda: kvbuf[k, n, :, :HD], lambda: kvbuf[k, n, :, HD:], window_bias(n, dt, dh, there), False, tiles)

    def text_cols(g, n):
        return tall[:, :, g * PART + n * HD:g * PART + (n + 1) * HD].reshape(256, HD)

    lane = lax.broadcasted_iota(jnp.int32, (16, HD), 1)

    def text_part(i, carry):
        blocks = pl.ds(i * 8, 8)
        stat = jnp.zeros((128, HD), F32)
        lanes = lax.broadcasted_iota(jnp.int32, (128, HD), 1)
        for n in range(3):
            tq = tall[blocks, :, n * HD:(n + 1) * HD].reshape(128, HD)
            t = lax.dot_general(tq, kv[n, :, :HD], (((1,), (1,)), ((), ())),
                                preferred_element_type=F32) * SCALE2
            peak = jnp.max(t, axis=1, keepdims=True)
            p = jnp.exp2(t - peak).astype(BF)
            both = jnp.dot(p, with_ones(kv[n, :, HD:]), preferred_element_type=F32)
            ts[blocks, :, n * HD:(n + 1) * HD] = (both[:, :HD] / both[:, HD:]).astype(BF).reshape(8, 16, HD)
            level = peak + jnp.log2(both[:, HD:])
            for e in range(3):
                piece_of = level.astype(BF).astype(F32)
                stat = jnp.where(lanes == 3 * e + n, piece_of, stat)
                level = level - piece_of
        ts[blocks, :, PART:] = stat.astype(BF).reshape(8, 16, HD)
        return carry

    text_row = jnp.where(lax.broadcasted_iota(jnp.int32, (1, 256), 1) < text_len[0], 0.0, NEG_BIG)

    def attend_text(n):
        attend(n, lambda: text_cols(1, n), lambda: text_cols(2, n), lambda i: text_row)

    chunks = ((0, 0, ROWS), (1, 0, ROWS), (2, 0, 384), (2, 384, 256))

    def ring_view(place, k, half):
        n, base, size = chunks[k]
        if half:
            size = size // 2
            base = base + (size if half == "b" else 0)
        return attbuf.at[places[place], n, pl.ds(base, size)]

    def ring_push(place, n, half, kind, to):
        ref = ring_view(place, n, half)
        cp = remote(ref, ref, zsend.at[RID[kind], n], zrecv.at[RID[kind], n], None, to)
        cp.start()
        sent.append(cp)

    def ring_arrive(place, n, half, kind):
        ref = ring_view(place, n, half)
        remote(ref, ref, zsend.at[RID[kind], n], zrecv.at[RID[kind], n], None, up).wait_recv()

    def close_head(k):
        n, base, size = chunks[k]

        def tile(i, carry):
            rows = pl.ds(i * 128, 128)
            attbuf[pl.ds(h, 1), n, rows, :] = (
                att[n, rows, :HD] / att[n, rows, HD:]).astype(BF).reshape(1, 128, HD)
            return carry

        lax.fori_loop(base // 128, (base + size) // 128, tile, 0, unroll=True)
        ring_push("O", k, "", "H", hn)
        ring_push("O", k, "", "Dn", up)
        ring_push("O", k, "", "Up", dn)

    def ring_one(n):
        ring_arrive("Dn", n, "", "Dn")
        ring_push("Dn", n, "a", "D2a", up)
        ring_arrive("Up", n, "", "Up")
        ring_push("Up", n, "b", "D2b", dn)
        ring_arrive("H", n, "", "H")
        ring_push("H", n, "", "HDn", up)
        ring_push("H", n, "", "HUp", dn)

    def ring_two(n):
        for half in ("a", "b"):
            ring_arrive("D2", n, half, "D2" + half)
            ring_push("D2", n, half, "HD2" + half, hn)

    def ring_three(n):
        ring_arrive("HDn", n, "", "HDn")
        ring_arrive("HUp", n, "", "HUp")
        for half in ("a", "b"):
            ring_arrive("HD2", n, half, "HD2" + half)

    def project(k):
        n, base, size = chunks[k]
        rows = pl.ds(base, size)
        for j in range(0, 8, 2):
            rhs = jnp.concatenate(
                [jnp.concatenate([wp[:, core, j + e, n].reshape(HD, SHARD) for core in range(2)], axis=1)
                 for e in range(2)], axis=0)
            lhs = jnp.concatenate([attbuf[j, n, rows], attbuf[j + 1, n, rows]], axis=1)
            term = jnp.dot(lhs, rhs, preferred_element_type=F32)
            if n == 0 and j == 0:
                acc2[rows, :] = term
            else:
                acc2[rows, :] += term

    def attend_own(n):
        attend(n, lambda: kv[n, :, :HD], lambda: kv[n, :, HD:], window_bias(n, 0, 0, None), True)

    def attend_other(k, n):
        if k != 1:
            kv_arrive(k, n)
        attend_block(k, n)

    finish(0)
    across.wait()
    part[pl.ds(c, 1), pl.ds(y * 4, 4)] = (
        part[pl.ds(c, 1), pl.ds(y * 4, 4)] + tsum_in[0:4].reshape(1, 4, 16, WIDE))
    along = []
    for d in range(1, 4):
        xo = (x + d) % 4
        along.append(remote(part.at[c, y * 4 + xo], tsum_in.at[4 + d], rsend.at[1 + d],
                            rrecv.at[1 + d], seq_of(y, xo, c)))
        along[-1].start()
    attend_own(0)
    multiply(1, "LY")
    multiply(1, "RY")
    multiply(1, "D")
    keep[2].wait()
    multiply(2, "O", True)
    multiply(2, "Y")
    multiply(2, "L")
    multiply(2, "R")
    wg[2].two()
    for cp in along:
        cp.wait()
    total = part[pl.ds(c, 1), pl.ds(chip, 1)].reshape(16, WIDE)
    for d in range(5, 8):
        total = total + tsum_in[d]
    for n in range(6):
        hd = total[:, n * HD:(n + 1) * HD]
        tall[pl.ds(s, 1), :, n * HD:(n + 1) * HD] = head_normed(
            hd, gaint[pl.ds(n // 3, 1), :]).astype(BF).reshape(1, 16, HD)
    tall[pl.ds(s, 1), :, 768:] = total[:, 768:].astype(BF).reshape(1, 16, PART)

    def text_block(yy, d, core):
        return tall.at[seq_of(yy, (x + 4 - d) % 4, core)]

    def text_push(k, block, to):
        cp = remote(block, block, gsend.at[k], grecv.at[k], to)
        cp.start()
        sent.append(cp)

    def text_arrive(k, block):
        remote(block, block, gsend.at[k], grecv.at[k], partner).wait_recv()

    for d in range(1, 4):
        text_push(d, text_block(y, 0, c), seq_of(y, (x + d) % 4, c))
    text_push(4, text_block(y, 0, c), ynbr)
    text_push(0, text_block(y, 0, c), partner)
    wg[1].three()
    multiply(1, "DY")
    finish(1)
    kv_forward(0)

    attend_own(1)
    attend_other(0, 0)
    attend_other(1, 0)
    multiply(2, "LY")
    multiply(2, "RY")
    multiply(2, "D")
    wg[2].three()
    multiply(2, "DY")
    finish(2)
    for d in range(1, 4):
        text_arrive(d, text_block(y, d, c))
        text_push(4 + d, text_block(y, d, c), ynbr)
        text_push(7 + d, text_block(y, d, c), partner)
    attend_own(2)
    attend_other(0, 1)
    attend_other(2, 0)
    attend_other(3, 0)
    kv_forward(1)
    for d in range(4):
        text_arrive(4 + d, text_block(1 - y, d, c))
        text_push(11 + d, text_block(1 - y, d, c), partner)
    attend_other(1, 1)
    for d in range(4):
        text_arrive(0 if d == 0 else 7 + d, text_block(y, d, 1 - c))
        text_arrive(11 + d, text_block(1 - y, d, 1 - c))

    attend_text(0)
    lax.fori_loop(0, 2, text_part, 0, unroll=True)

    def merge_send(d, carry):
        to = (s + d) % 16
        remote(ts.at[to], ts_in.at[d], msend.at[d], mrecv.at[d], to).start()
        return carry

    lax.fori_loop(1, 16, merge_send, 0)
    attend_other(4, 0)
    close_head(0)
    attend_text(1)
    def piece(j, carry):
        @pl.when(jnp.logical_not(jnp.logical_and(s // 2 == h, j == h)))
        def _():
            remote(wp.at[0, 0, 0], wp.at[chip, c, j], wsend.at[0], wrecv.at[j], partner).wait_recv()
        return carry

    lax.fori_loop(0, 8, piece, 0)

    @pl.when(home == 1)
    def _():
        pltpu.make_async_copy(pv.at[:, 0], wp.at[chip, c, h], own_sem.at[2]).wait()

    pg.own()
    attend_other(2, 1)
    attend_other(3, 1)
    kv_forward(2)
    attend_other(0, 2)
    attend_other(1, 2)
    attend_text(2)
    ring_one(0)
    attend_other(4, 1)
    close_head(1)
    pg.one()
    attend_other(2, 2)
    attend_other(3, 2)
    ring_two(0)
    kv_arrive(4, 2)
    attend_block(4, 2, (0, 3))
    close_head(2)
    attend_block(4, 2, (3, TILES))
    close_head(3)
    ring_one(1)
    pg.two()
    def merge_wait(d, carry):
        remote(ts.at[0], ts_in.at[d], msend.at[d], mrecv.at[d], partner).wait_recv()
        return carry

    lax.fori_loop(1, 16, merge_wait, 0)
    ts_in[0] = ts[pl.ds(s, 1)].reshape(16, 512)
    levels = [ts_in[d, :, PART:].astype(F32) for d in range(16)]
    for n in range(3):
        tq = tall[pl.ds(s, 1), :, n * HD:(n + 1) * HD].reshape(16, HD)
        t = lax.dot_general(tq, text_cols(1, n), (((1,), (1,)), ((), ())),
                            preferred_element_type=F32) * SCALE2 + text_row
        peak = jnp.max(t, axis=1, keepdims=True)
        p = jnp.exp2(t - peak).astype(BF)
        both = jnp.dot(p, with_ones(text_cols(2, n)), preferred_element_type=F32)
        logs = [v[:, n:n + 1] + v[:, n + 3:n + 4] + v[:, n + 6:n + 7] for v in levels]
        high = peak + jnp.log2(both[:, HD:HD + 1])
        for value in logs:
            high = jnp.maximum(high, value)
        weight = jnp.exp2(peak - high)
        upper = both[:, :HD] * weight
        lower = both[:, HD:HD + 1] * weight
        for d in range(16):
            weight = jnp.exp2(logs[d] - high)
            upper = upper + ts_in[d, :, n * HD:(n + 1) * HD].astype(F32) * weight
            lower = lower + weight
        atg[pl.ds(s, 1), :, n * HD:(n + 1) * HD] = (upper / lower).astype(BF).reshape(1, 16, HD)

    def text_give(d, carry):
        remote(atg.at[s], atg.at[s], asend.at[d], arecv.at[d], (s + d) % 16).start()
        return carry

    lax.fori_loop(1, 16, text_give, 0)

    ring_one(2)
    ring_two(1)
    ring_one(3)
    ring_two(2)
    pg.three()
    fetch_pt.wait()
    def text_given(d, carry):
        block = atg.at[(s + 16 - d) % 16]
        remote(block, block, asend.at[d], arecv.at[d], partner).wait_recv()
        return carry

    lax.fori_loop(1, 16, text_given, 0)
    tpart[...] = lax.dot_general(
        atg[...].reshape(256, PART), pt[...], (((1,), (1,)), ((), ())),
        preferred_element_type=F32).reshape(16, 16, SHARD)

    def text_move(i, carry):
        here = jnp.logical_and(i == s, s // 2 == h)

        @pl.when(jnp.logical_not(here))
        def _():
            remote(tpart.at[i], tpart_in.at[c, h], osend.at[i], orecv.at[c, h], i, s // 2).start()

        @pl.when(here)
        def _():
            pltpu.make_async_copy(tpart.at[i], tpart_in.at[c, h], own_sem.at[3]).start()
        return carry

    lax.fori_loop(0, 16, text_move, 0)

    ring_two(3)
    for place in ("O", "Y", "L", "R", "LY", "RY", "D", "DY"):
        pg.pair(place)
    ring_three(0)
    project(0)
    ring_three(1)
    project(1)
    ring_three(2)
    project(2)

    def text_moved(i, carry):
        @pl.when(jnp.logical_not(jnp.logical_and(2 * h + i % 2 == s, i // 2 == h)))
        def _():
            remote(tpart.at[0], tpart_in.at[i % 2, i // 2], osend.at[0], orecv.at[i % 2, i // 2],
                   partner).wait_recv()
        return carry

    lax.fori_loop(0, 16, text_moved, 0)

    @pl.when(home == 1)
    def _():
        pltpu.make_async_copy(tpart.at[0], tpart_in.at[c, h], own_sem.at[3]).wait()

    out_cols = pl.ds(pl.multiple_of(h * PART, PART), PART)
    sums = jnp.concatenate([jnp.sum(tpart_in[0], axis=0), jnp.sum(tpart_in[1], axis=0)], axis=1)
    text_out[...] = (txt[:, out_cols].astype(F32) + modt[pl.ds(2, 1), out_cols] * sums).astype(BF)

    ring_three(3)
    project(3)
    gate = modv[pl.ds(2, 1), out_cols]

    def write(i, carry):
        rows = pl.ds(pl.multiple_of(i * 16, 16), 16)
        at = pl.ds(pl.multiple_of(((i % TILES) * 8 + i // TILES) * 16, 16), 16)
        video_out[rows, :] = (vid[rows, out_cols].astype(F32) + gate * acc2[at, :]).astype(BF)
        return carry

    lax.fori_loop(0, 40, write, 0, unroll=4)

    def left_t(d, carry):
        remote(nt.at[0], tnt.at[0], tsend.at[d], trecv.at[d], partner).wait_send()
        remote(ts.at[0], ts_in.at[0], msend.at[d], mrecv.at[d], partner).wait_send()
        remote(atg.at[0], atg.at[0], asend.at[d], arecv.at[d], partner).wait_send()
        return carry

    lax.fori_loop(1, 16, left_t, 0)

    def left_w(j, carry):
        @pl.when(jnp.logical_not(jnp.logical_and(2 * j + c == s, s // 2 == h)))
        def _():
            remote(pv.at[:, 0], wp.at[0, 0, 0], wsend.at[j], wrecv.at[0], partner).wait_send()
        return carry

    lax.fori_loop(0, 8, left_w, 0)

    def left_o(i, carry):
        @pl.when(jnp.logical_not(jnp.logical_and(i == s, s // 2 == h)))
        def _():
            remote(tpart.at[0], tpart_in.at[0, 0], osend.at[i], orecv.at[0, 0], partner).wait_send()
        return carry

    lax.fori_loop(0, 16, left_o, 0)
    for cp in sent:
        cp.wait_send()


def block_kernel(vid, txt, modv, modt, w, wt, pv, pt, gainv, gaint, windows, text_len):
    vm = pl.BlockSpec(memory_space=pltpu.VMEM)
    sm = pl.BlockSpec(memory_space=pltpu.SMEM)
    hbm = pl.BlockSpec(memory_space=pl.ANY)
    dma = pltpu.SemaphoreType.DMA
    v = pltpu.VMEM
    return pl.pallas_call(
        kernel,
        name="attention_block",
        out_shape=(jax.ShapeDtypeStruct((ROWS, PART), BF), jax.ShapeDtypeStruct((16, PART), BF)),
        in_specs=[hbm] + [vm] * 3 + [hbm] * 4 + [vm] * 2 + [sm, sm],
        out_specs=(vm, vm),
        scratch_shapes=[
            v((ROWS, 3072), BF), v((3, SHARD, PART), BF), v((SHARD, PART), BF), v((SHARD, PART), BF),
            v((3, 8, 16, SHARD), BF),
            v((ROWS, 3072), BF), v((3, 8, 2, 3, SHARD, HD), BF), v((3, ROWS, PART), F32),
            v((16, 16, SHARD), BF), v((16, 16, SHARD), BF),
            v((2, 8, 16, WIDE), F32), v((8, 16, WIDE), F32), v((8, 16, WIDE), F32),
            v((16, 16, WIDE), BF),
            v((3, ROWS, HD), BF), v((3, ROWS, 2 * HD), BF), v((5, 3, ROWS, 2 * HD), BF),
            v((3, ROWS, HD), F32), v((3, ROWS, 2 * HD), F32), v((8, 3, ROWS, HD), BF),
            v((8, 2, 8, 3, 16, SHARD), BF), v((ROWS, PART), F32),
            v((16, 16, 512), BF), v((16, 16, 512), BF), v((16, 16, PART), BF),
            v((16, 16, SHARD), F32), v((2, 8, 16, SHARD), F32),
            dma((11,)), dma((3, 19)), dma((3, 19)), dma((16,)), dma((16,)),
            dma((8,)), dma((8,)), dma((15,)), dma((15,)),
            dma((5, 3)), dma((5, 3)), dma((9, 4)), dma((9, 4)),
            dma((8,)), dma((8,)), dma((19,)), dma((19,)),
            dma((16,)), dma((16,)), dma((16,)), dma((16,)), dma((16,)), dma((2, 8)),
        ],
        compiler_params=pltpu.CompilerParams(
            collective_id=1, has_side_effects=True, vmem_limit_bytes=58 * 2**20),
    )(vid, txt, modv, modt, w, wt, pv, pt, gainv, gaint, windows, text_len)


def body(video_in, text_in, mod_video, mod_text, qkv_video, qkv_text, proj_video, proj_text,
         gain_video, gain_text, windows, text_len):
    return block_kernel(
        video_in, text_in, mod_video, mod_text,
        jnp.transpose(qkv_video, (1, 0, 2)), jnp.transpose(qkv_text, (1, 0, 2)),
        proj_video.T, proj_text.T,
        gain_video, gain_text, windows.T, text_len)


def solution(mesh):
    return jax.shard_map(
        body,
        mesh=mesh,
        in_specs=(
            P("seq", None), P("seq", None), P(), P(),
            P("seq", None, "head"), P("seq", None, "head"),
            P("head", "seq"), P("head", "seq"), P(), P(), P(), P(),
        ),
        out_specs=(P("seq", "head"), P("seq", "head")),
        check_vma=False,
    )
```

```python
import math

import jax
import jax.numpy as jnp
from jax import lax
from jax.experimental import pallas as pl
from jax.experimental.pallas import tpu as pltpu
from jax.sharding import PartitionSpec as P

MESH = pl.DeviceIdType.MESH
BF = jnp.bfloat16
F32 = jnp.float32
ROWS = 640
WIDE = 1152
PART = 384
SHARD = 192
HD = 128
TILES = 5
NEG_BIG = -1e30
SCALE2 = math.log2(math.e) / math.sqrt(HD)

GATHER = ("PO", "Y", "L", "R", "LY", "RY", "Da", "Db", "DYa", "DYb",
          "PY", "PL", "PR", "PLY", "PRY", "PDa", "PDb", "PDYa", "PDYb")
GID = {k: i for i, k in enumerate(GATHER)}
RING = ("Up", "Dn", "H", "HUp", "HDn", "D2a", "D2b", "HD2a", "HD2b")
RID = {k: i for i, k in enumerate(RING)}


def remote(src, dst, send, recv, seq=None, head=None):
    to = {}
    if seq is not None:
        to["seq"] = seq
    if head is not None:
        to["head"] = head
    return pltpu.make_async_remote_copy(
        src_ref=src, dst_ref=dst, send_sem=send, recv_sem=recv,
        device_id=to, device_id_type=MESH)


def head_normed(vals, gain):
    return vals * lax.rsqrt(jnp.mean(jnp.square(vals), axis=1, keepdims=True) + 1e-6) * gain


def with_ones(value):
    return jnp.concatenate([value, jnp.ones_like(value)], axis=1)


def kernel(vid_hbm, txt, modv, modt, w, wt_hbm, pv_hbm, pt_hbm, gainv, gaint, windows, text_len,
           video_out, text_out,
           vid, wt, pvt, pt, pv, normed, wbuf, acc, nt, tnt, part, ppart, tsum_in, tall,
           q, kv, kvbuf, top, att, attbuf, wp, acc2,
           ts, ts_in, atg, tpart, tpart_in,
           own_sem, send, recv, tsend, trecv, rsend, rrecv, gsend, grecv,
           ksend, krecv, zsend, zrecv, wsend, wrecv, psend, precv,
           msend, mrecv, asend, arecv, osend, orecv):
    s = lax.axis_index("seq")
    h = lax.axis_index("head")
    y, x, c = s // 8, (s % 8) // 2, s % 2
    z, yh = h % 4, h // 4
    chip = y * 4 + x

    def seq_of(y, x, c):
        return y * 8 + x * 2 + c

    partner = seq_of(y, x, 1 - c)
    ynbr = seq_of(1 - y, x, c)
    xl, xr, xd = (x + 3) % 4, (x + 1) % 4, (x + 2) % 4
    left, right = seq_of(y, xl, c), seq_of(y, xr, c)
    xnbr = seq_of(y, (x + 3 + 2 * c) % 4, 1 - c)
    slots = {"O": chip, "Y": (1 - y) * 4 + x, "L": y * 4 + xl, "R": y * 4 + xr,
             "LY": (1 - y) * 4 + xl, "RY": (1 - y) * 4 + xr,
             "D": y * 4 + xd, "DY": (1 - y) * 4 + xd}
    up, dn, hn = yh * 4 + (z + 1) % 4, yh * 4 + (z + 3) % 4, (1 - yh) * 4 + z
    places = {"O": h, "Up": up, "Dn": dn, "H": hn,
              "HUp": (1 - yh) * 4 + (z + 1) % 4, "HDn": (1 - yh) * 4 + (z + 3) % 4,
              "D2": yh * 4 + (z + 2) % 4, "HD2": (1 - yh) * 4 + (z + 2) % 4}
    home = jnp.where(h == s // 2, 1, 0)

    def fetch(i, src, dst):
        cp = pltpu.make_async_copy(src, dst, own_sem.at[i])
        cp.start()
        return cp

    def shard(n):
        return w.at[:, :, pl.ds(n * HD, HD)]

    fetch_vid = fetch(4, vid_hbm, vid)
    fetch_pv = fetch(5, pv_hbm, pvt)
    fetch_wt = fetch(6, wt_hbm, wt)
    fetch_pt = fetch(7, pt_hbm, pt)
    keep = [fetch(8 + n, shard(n), wbuf.at[n, chip, c]) for n in range(3)]

    barrier = pltpu.get_barrier_semaphore()

    def greet(d, carry):
        pl.semaphore_signal(barrier, inc=1, device_id={"seq": (s + d) % 16}, device_id_type=MESH)
        return carry

    lax.fori_loop(1, 16, greet, 0)
    for peer in (up, dn, hn):
        pl.semaphore_signal(barrier, inc=1, device_id={"head": peer}, device_id_type=MESH)

    def greet_far(i, carry):
        far_s, far_h = 2 * h + i % 2, i // 2

        @pl.when(jnp.logical_or(far_s != s, far_h != h))
        def _():
            pl.semaphore_signal(barrier, inc=1, device_id={"seq": far_s, "head": far_h},
                                device_id_type=MESH)
        return carry

    lax.fori_loop(0, 16, greet_far, 0)
    def layer_norm(vals, shift, scale):
        vals = vals.astype(F32)
        vals = vals - jnp.mean(vals, axis=1, keepdims=True)
        spread = jnp.mean(jnp.square(vals), axis=1, keepdims=True)
        return (vals * lax.rsqrt(spread + 1e-6) * scale + shift).astype(BF)

    text_normed = layer_norm(txt[...], modt[pl.ds(0, 1), :], 1.0 + modt[pl.ds(1, 1), :])
    for d in range(16):
        nt[d] = text_normed[:, d * SHARD:(d + 1) * SHARD]
    pl.semaphore_wait(barrier, 15 + 3 + 16 - home)

    sent = []

    class Gather:
        def __init__(self, at, ssem, rsem, cut):
            self.at, self.ssem, self.rsem, self.cut = at, ssem, rsem, cut

        def view(self, place, core, half):
            ref = self.at(slots[place], core)
            return self.cut(ref, half) if half else ref

        def push(self, place, core, half, kind, to, src=None):
            ref = self.view(place, core, half)
            cp = remote(ref if src is None else src, ref, self.ssem.at[GID[kind]],
                        self.rsem.at[GID[kind]], to)
            cp.start()
            sent.append(cp)

        def arrive(self, place, core, half, kind):
            ref = self.view(place, core, half)
            remote(ref, ref, self.ssem.at[GID[kind]], self.rsem.at[GID[kind]], partner).wait_recv()

        def own(self, src=None):
            self.push("O", c, "", "L", right, src)
            self.push("O", c, "", "R", left, src)
            self.push("O", c, "", "Y", ynbr, src)
            self.push("O", c, "", "PO", partner, src)

        def one(self):
            self.arrive("L", c, "", "L")
            self.push("L", c, "a", "Da", right)
            self.arrive("R", c, "", "R")
            self.push("R", c, "b", "Db", left)
            self.arrive("Y", c, "", "Y")
            self.push("Y", c, "", "RY", left)
            self.push("Y", c, "", "LY", right)
            self.push("L", c, "", "PL", partner)
            self.push("R", c, "", "PR", partner)
            self.push("Y", c, "", "PY", partner)

        def two(self):
            for half in ("a", "b"):
                self.arrive("D", c, half, "D" + half)
                self.push("D", c, half, "DY" + half, ynbr)
                self.push("D", c, half, "PD" + half, partner)
            for place in ("LY", "RY"):
                self.arrive(place, c, "", place)
                self.push(place, c, "", "P" + place, partner)

        def three(self):
            for half in ("a", "b"):
                self.arrive("DY", c, half, "DY" + half)
                self.push("DY", c, half, "PDY" + half, partner)

        def pair(self, place):
            if place in ("D", "DY"):
                for half in ("a", "b"):
                    self.arrive(place, 1 - c, half, "P" + place + half)
            else:
                self.arrive(place, 1 - c, "", "P" + place)

    def cut_weights(ref, half):
        return ref.at[:, pl.ds(0 if half == "a" else SHARD // 2, SHARD // 2)]

    def cut_pieces(ref, half):
        return ref.at[pl.ds(0 if half == "a" else 4, 4)]

    wg = [Gather(lambda j, core, n=n: wbuf.at[n, j, core], send.at[n], recv.at[n], cut_weights)
          for n in range(3)]
    pg = Gather(lambda j, core: wp.at[j, core], psend, precv, cut_pieces)

    wg[0].own(shard(0))

    own_row = c * 8 + chip

    def scatter(d, carry):
        to = (s + d) % 16
        remote(nt.at[to], tnt.at[own_row], tsend.at[d], trecv.at[d], to).start()
        return carry

    lax.fori_loop(1, 16, scatter, 0)
    keep_t = pltpu.make_async_copy(nt.at[s], tnt.at[own_row], own_sem.at[1])
    keep_t.start()
    wg[1].own(shard(1))

    shift = modv[pl.ds(0, 1), :]
    scale = 1.0 + modv[pl.ds(1, 1), :]

    def norm_rows(i, carry):
        to = (i % TILES) * 8 + i // TILES
        normed[pl.ds(pl.multiple_of(to * 16, 16), 16), :] = layer_norm(
            vid[pl.ds(pl.multiple_of(i * 16, 16), 16), :], shift, scale)
        return carry

    fetch_vid.wait()
    lax.fori_loop(0, 40, norm_rows, 0, unroll=4)
    wg[0].one()

    def scattered(d, carry):
        remote(nt.at[0], tnt.at[0], tsend.at[d], trecv.at[d], partner).wait_recv()
        return carry

    lax.fori_loop(1, 16, scattered, 0)
    keep_t.wait()
    fetch_wt.wait()
    for g in range(3):
        part[:, :, :, g * PART:(g + 1) * PART] = jnp.dot(
            tnt[...].reshape(256, SHARD), wt[g], preferred_element_type=F32
        ).reshape(2, 8, 16, PART)
    swap = remote(part.at[1 - c], ppart, rsend.at[0], rrecv.at[0], partner)
    swap.start()
    wg[2].own(shard(2))
    fetch_pv.wait()
    pv[...] = pvt[...].astype(F32).T.astype(BF).reshape(3, 8, 16, SHARD)

    def pieces(j, carry):
        to_s, to_h = 2 * j + c, s // 2
        here = jnp.logical_and(to_s == s, to_h == h)

        @pl.when(jnp.logical_not(here))
        def _():
            remote(pv.at[:, j], wp.at[j, c, h], wsend.at[j], wrecv.at[h], to_s, to_h).start()

        @pl.when(here)
        def _():
            pltpu.make_async_copy(pv.at[:, j], wp.at[j, c, h], own_sem.at[2]).start()
        return carry

    lax.fori_loop(0, 8, pieces, 0)

    def multiply(n, place, first=False):
        wg[n].pair(place)
        j = slots[place]
        lhs = normed[:, pl.ds(pl.multiple_of(j * PART, PART), PART)]
        rhs = jnp.concatenate([wbuf[n, j, :, g].reshape(PART, HD) for g in range(3)], axis=1)
        term = jnp.dot(lhs, rhs, preferred_element_type=F32)
        if first:
            acc[n] = term
        else:
            acc[n] += term

    keep[0].wait()
    multiply(0, "O", True)
    swap.wait()
    part[pl.ds(c, 1)] = part[pl.ds(c, 1)] + ppart[...].reshape(1, 8, 16, WIDE)

    across = remote(part.at[c, pl.ds((1 - y) * 4, 4)], tsum_in.at[pl.ds(0, 4)],
                    rsend.at[1], rrecv.at[1], ynbr)
    across.start()
    wg[1].one()
    multiply(0, "Y")
    multiply(0, "L")
    multiply(0, "R")
    wg[0].two()
    keep[1].wait()
    multiply(1, "O", True)
    wg[2].one()
    multiply(0, "LY")
    multiply(0, "RY")
    multiply(0, "D")
    multiply(1, "Y")
    multiply(1, "L")
    multiply(1, "R")
    wg[1].two()
    wg[0].three()
    multiply(0, "DY")
    def kv_push(k, n, to, src=None):
        src = kv.at[n] if src is None else src
        cp = remote(src, kvbuf.at[k, n], ksend.at[k, n], krecv.at[k, n], to)
        cp.start()
        sent.append(cp)

    def kv_arrive(k, n):
        ref = kvbuf.at[k, n]
        remote(ref, ref, ksend.at[k, n], krecv.at[k, n], partner).wait_recv()

    def finish(n):
        def keys(i, carry):
            rows = pl.ds(i * 128, 128)
            kv[n, rows, :HD] = head_normed(acc[n, rows, HD:2 * HD], gainv[pl.ds(1, 1), :]).astype(BF)
            kv[n, rows, HD:] = acc[n, rows, 2 * HD:].astype(BF)
            return carry

        def queries(i, carry):
            rows = pl.ds(i * 128, 128)
            q[n, rows] = head_normed(acc[n, rows, :HD], gainv[pl.ds(0, 1), :]).astype(BF)
            return carry

        lax.fori_loop(0, TILES, keys, 0, unroll=True)
        kv_push(1, n, ynbr)
        kv_push(3, n, xnbr)
        kv_push(0, n, partner)
        lax.fori_loop(0, TILES, queries, 0, unroll=True)

    def kv_forward(n):
        kv_arrive(1, n)
        kv_push(4, n, xnbr, kvbuf.at[1, n])
        kv_push(2, n, partner, kvbuf.at[1, n])

    height = 2 * x + c
    x_there = jnp.where(jnp.logical_or(jnp.logical_and(height == 0, c == 0),
                                       jnp.logical_and(height == 7, c == 1)), 0, 1)
    lane_tile = lax.broadcasted_iota(jnp.int32, (1, ROWS), 1) // 128

    def attend(n, keys, values, bias_of, first=False, tiles=(0, TILES)):
        def tile(i, carry):
            rows = pl.ds(pl.multiple_of(i * 128, 128), 128)
            t = lax.dot_general(q[n, rows], keys(), (((1,), (1,)), ((), ())),
                                preferred_element_type=F32) * SCALE2 + bias_of(i)
            peak = jnp.max(t, axis=1, keepdims=True)
            if first:
                new = peak
            else:
                old = top[n, rows, :]
                new = jnp.maximum(old, peak)
            p = jnp.exp2(t - new[:, :1]).astype(BF)
            gain = jnp.dot(p, with_ones(values()), preferred_element_type=F32)
            if first:
                att[n, rows, :] = gain
            else:
                factor = jnp.exp2(old - new)
                att[n, rows, :] = att[n, rows, :] * jnp.concatenate([factor, factor], axis=1) + gain
            top[n, rows, :] = jnp.broadcast_to(new, (128, HD))
            return carry

        lax.fori_loop(*tiles, tile, 0, unroll=True)

    def window_bias(n, dt, dh, there):
        row = h * 3 + n
        fits = jnp.logical_and(windows[0, row] >= dt, windows[1, row] >= dh)
        reach = jnp.where(fits, windows[2, row], -1)
        if there is not None:
            reach = jnp.where(there == 1, reach, -1)
        return lambda i: jnp.where(jnp.abs(lane_tile - i) <= reach, 0.0, NEG_BIG)

    def attend_block(k, n, tiles=(0, TILES)):
        dt = 1 if k in (1, 2, 4) else 0
        dh = 1 if k in (0, 2, 3, 4) else 0
        there = x_there if k in (3, 4) else None
        attend(n, lambda: kvbuf[k, n, :, :HD], lambda: kvbuf[k, n, :, HD:], window_bias(n, dt, dh, there), False, tiles)

    def text_cols(g, n):
        return tall[:, :, g * PART + n * HD:g * PART + (n + 1) * HD].reshape(256, HD)

    lane = lax.broadcasted_iota(jnp.int32, (16, HD), 1)

    def text_part(i, carry):
        blocks = pl.ds(i * 8, 8)
        stat = jnp.zeros((128, HD), F32)
        lanes = lax.broadcasted_iota(jnp.int32, (128, HD), 1)
        for n in range(3):
            tq = tall[blocks, :, n * HD:(n + 1) * HD].reshape(128, HD)
            t = lax.dot_general(tq, kv[n, :, :HD], (((1,), (1,)), ((), ())),
                                preferred_element_type=F32) * SCALE2
            peak = jnp.max(t, axis=1, keepdims=True)
            p = jnp.exp2(t - peak).astype(BF)
            both = jnp.dot(p, with_ones(kv[n, :, HD:]), preferred_element_type=F32)
            ts[blocks, :, n * HD:(n + 1) * HD] = (both[:, :HD] / both[:, HD:]).astype(BF).reshape(8, 16, HD)
            level = peak + jnp.log2(both[:, HD:])
            for e in range(3):
                piece_of = level.astype(BF).astype(F32)
                stat = jnp.where(lanes == 3 * e + n, piece_of, stat)
                level = level - piece_of
        ts[blocks, :, PART:] = stat.astype(BF).reshape(8, 16, HD)
        return carry

    text_row = jnp.where(lax.broadcasted_iota(jnp.int32, (1, 256), 1) < text_len[0], 0.0, NEG_BIG)

    def attend_text(n):
        attend(n, lambda: text_cols(1, n), lambda: text_cols(2, n), lambda i: text_row)

    chunks = ((0, 0, ROWS), (1, 0, ROWS), (2, 0, 384), (2, 384, 256))

    def ring_view(place, k, half):
        n, base, size = chunks[k]
        if half:
            size = size // 2
            base = base + (size if half == "b" else 0)
        return attbuf.at[places[place], n, pl.ds(base, size)]

    def ring_push(place, n, half, kind, to):
        ref = ring_view(place, n, half)
        cp = remote(ref, ref, zsend.at[RID[kind], n], zrecv.at[RID[kind], n], None, to)
        cp.start()
        sent.append(cp)

    def ring_arrive(place, n, half, kind):
        ref = ring_view(place, n, half)
        remote(ref, ref, zsend.at[RID[kind], n], zrecv.at[RID[kind], n], None, up).wait_recv()

    def close_head(k):
        n, base, size = chunks[k]

        def tile(i, carry):
            rows = pl.ds(i * 128, 128)
            attbuf[pl.ds(h, 1), n, rows, :] = (
                att[n, rows, :HD] / att[n, rows, HD:]).astype(BF).reshape(1, 128, HD)
            return carry

        lax.fori_loop(base // 128, (base + size) // 128, tile, 0, unroll=True)
        ring_push("O", k, "", "H", hn)
        ring_push("O", k, "", "Dn", up)
        ring_push("O", k, "", "Up", dn)

    def ring_one(n):
        ring_arrive("Dn", n, "", "Dn")
        ring_push("Dn", n, "a", "D2a", up)
        ring_arrive("Up", n, "", "Up")
        ring_push("Up", n, "b", "D2b", dn)
        ring_arrive("H", n, "", "H")
        ring_push("H", n, "", "HDn", up)
        ring_push("H", n, "", "HUp", dn)

    def ring_two(n):
        for half in ("a", "b"):
            ring_arrive("D2", n, half, "D2" + half)
            ring_push("D2", n, half, "HD2" + half, hn)

    def ring_three(n):
        ring_arrive("HDn", n, "", "HDn")
        ring_arrive("HUp", n, "", "HUp")
        for half in ("a", "b"):
            ring_arrive("HD2", n, half, "HD2" + half)

    def project(k):
        n, base, size = chunks[k]
        rows = pl.ds(base, size)
        for j in range(0, 8, 2):
            rhs = jnp.concatenate(
                [jnp.concatenate([wp[:, core, j + e, n].reshape(HD, SHARD) for core in range(2)], axis=1)
                 for e in range(2)], axis=0)
            lhs = jnp.concatenate([attbuf[j, n, rows], attbuf[j + 1, n, rows]], axis=1)
            term = jnp.dot(lhs, rhs, preferred_element_type=F32)
            if n == 0 and j == 0:
                acc2[rows, :] = term
            else:
                acc2[rows, :] += term

    def attend_own(n):
        attend(n, lambda: kv[n, :, :HD], lambda: kv[n, :, HD:], window_bias(n, 0, 0, None), True)

    def attend_other(k, n):
        if k != 1:
            kv_arrive(k, n)
        attend_block(k, n)

    finish(0)
    across.wait()
    part[pl.ds(c, 1), pl.ds(y * 4, 4)] = (
        part[pl.ds(c, 1), pl.ds(y * 4, 4)] + tsum_in[0:4].reshape(1, 4, 16, WIDE))
    along = []
    for d in range(1, 4):
        xo = (x + d) % 4
        along.append(remote(part.at[c, y * 4 + xo], tsum_in.at[4 + d], rsend.at[1 + d],
                            rrecv.at[1 + d], seq_of(y, xo, c)))
        along[-1].start()
    attend_own(0)
    multiply(1, "LY")
    multiply(1, "RY")
    multiply(1, "D")
    keep[2].wait()
    multiply(2, "O", True)
    multiply(2, "Y")
    multiply(2, "L")
    multiply(2, "R")
    wg[2].two()
    for cp in along:
        cp.wait()
    total = part[pl.ds(c, 1), pl.ds(chip, 1)].reshape(16, WIDE)
    for d in range(5, 8):
        total = total + tsum_in[d]
    for n in range(6):
        hd = total[:, n * HD:(n + 1) * HD]
        tall[pl.ds(s, 1), :, n * HD:(n + 1) * HD] = head_normed(
            hd, gaint[pl.ds(n // 3, 1), :]).astype(BF).reshape(1, 16, HD)
    tall[pl.ds(s, 1), :, 768:] = total[:, 768:].astype(BF).reshape(1, 16, PART)

    def text_block(yy, d, core):
        return tall.at[seq_of(yy, (x + 4 - d) % 4, core)]

    def text_push(k, block, to):
        cp = remote(block, block, gsend.at[k], grecv.at[k], to)
        cp.start()
        sent.append(cp)

    def text_arrive(k, block):
        remote(block, block, gsend.at[k], grecv.at[k], partner).wait_recv()

    for d in range(1, 4):
        text_push(d, text_block(y, 0, c), seq_of(y, (x + d) % 4, c))
    text_push(4, text_block(y, 0, c), ynbr)
    text_push(0, text_block(y, 0, c), partner)
    wg[1].three()
    multiply(1, "DY")
    finish(1)
    kv_forward(0)

    attend_own(1)
    attend_other(0, 0)
    attend_other(1, 0)
    multiply(2, "LY")
    multiply(2, "RY")
    multiply(2, "D")
    wg[2].three()
    multiply(2, "DY")
    finish(2)
    for d in range(1, 4):
        text_arrive(d, text_block(y, d, c))
        text_push(4 + d, text_block(y, d, c), ynbr)
        text_push(7 + d, text_block(y, d, c), partner)
    attend_own(2)
    attend_other(0, 1)
    attend_other(2, 0)
    attend_other(3, 0)
    kv_forward(1)
    for d in range(4):
        text_arrive(4 + d, text_block(1 - y, d, c))
        text_push(11 + d, text_block(1 - y, d, c), partner)
    attend_other(1, 1)
    for d in range(4):
        text_arrive(0 if d == 0 else 7 + d, text_block(y, d, 1 - c))
        text_arrive(11 + d, text_block(1 - y, d, 1 - c))

    attend_text(0)
    lax.fori_loop(0, 2, text_part, 0, unroll=True)

    def merge_send(d, carry):
        to = (s + d) % 16
        remote(ts.at[to], ts_in.at[d], msend.at[d], mrecv.at[d], to).start()
        return carry

    lax.fori_loop(1, 16, merge_send, 0)
    attend_other(4, 0)
    close_head(0)
    attend_text(1)
    def piece(j, carry):
        @pl.when(jnp.logical_not(jnp.logical_and(s // 2 == h, j == h)))
        def _():
            remote(wp.at[0, 0, 0], wp.at[chip, c, j], wsend.at[0], wrecv.at[j], partner).wait_recv()
        return carry

    lax.fori_loop(0, 8, piece, 0)

    @pl.when(home == 1)
    def _():
        pltpu.make_async_copy(pv.at[:, 0], wp.at[chip, c, h], own_sem.at[2]).wait()

    pg.own()
    attend_other(2, 1)
    attend_other(3, 1)
    kv_forward(2)
    attend_other(0, 2)
    attend_other(1, 2)
    attend_text(2)
    ring_one(0)
    attend_other(4, 1)
    close_head(1)
    pg.one()
    attend_other(2, 2)
    attend_other(3, 2)
    ring_two(0)
    def merge_wait(d, carry):
        remote(ts.at[0], ts_in.at[d], msend.at[d], mrecv.at[d], partner).wait_recv()
        return carry

    lax.fori_loop(1, 16, merge_wait, 0)
    ts_in[0] = ts[pl.ds(s, 1)].reshape(16, 512)
    levels = [ts_in[d, :, PART:].astype(F32) for d in range(16)]
    for n in range(3):
        tq = tall[pl.ds(s, 1), :, n * HD:(n + 1) * HD].reshape(16, HD)
        t = lax.dot_general(tq, text_cols(1, n), (((1,), (1,)), ((), ())),
                            preferred_element_type=F32) * SCALE2 + text_row
        peak = jnp.max(t, axis=1, keepdims=True)
        p = jnp.exp2(t - peak).astype(BF)
        both = jnp.dot(p, with_ones(text_cols(2, n)), preferred_element_type=F32)
        logs = [v[:, n:n + 1] + v[:, n + 3:n + 4] + v[:, n + 6:n + 7] for v in levels]
        high = peak + jnp.log2(both[:, HD:HD + 1])
        for value in logs:
            high = jnp.maximum(high, value)
        weight = jnp.exp2(peak - high)
        upper = both[:, :HD] * weight
        lower = both[:, HD:HD + 1] * weight
        for d in range(16):
            weight = jnp.exp2(logs[d] - high)
            upper = upper + ts_in[d, :, n * HD:(n + 1) * HD].astype(F32) * weight
            lower = lower + weight
        atg[pl.ds(s, 1), :, n * HD:(n + 1) * HD] = (upper / lower).astype(BF).reshape(1, 16, HD)

    def text_give(d, carry):
        remote(atg.at[s], atg.at[s], asend.at[d], arecv.at[d], (s + d) % 16).start()
        return carry

    lax.fori_loop(1, 16, text_give, 0)

    kv_arrive(4, 2)
    attend_block(4, 2, (0, 3))
    close_head(2)
    attend_block(4, 2, (3, TILES))
    close_head(3)
    ring_one(1)
    pg.two()
    fetch_pt.wait()
    def text_given(d, carry):
        block = atg.at[(s + 16 - d) % 16]
        remote(block, block, asend.at[d], arecv.at[d], partner).wait_recv()
        return carry

    lax.fori_loop(1, 16, text_given, 0)
    tpart[...] = lax.dot_general(
        atg[...].reshape(256, PART), pt[...], (((1,), (1,)), ((), ())),
        preferred_element_type=F32).reshape(16, 16, SHARD)

    def text_move(i, carry):
        here = jnp.logical_and(i == s, s // 2 == h)

        @pl.when(jnp.logical_not(here))
        def _():
            remote(tpart.at[i], tpart_in.at[c, h], osend.at[i], orecv.at[c, h], i, s // 2).start()

        @pl.when(here)
        def _():
            pltpu.make_async_copy(tpart.at[i], tpart_in.at[c, h], own_sem.at[3]).start()
        return carry

    lax.fori_loop(0, 16, text_move, 0)

    ring_one(2)
    ring_two(1)
    ring_one(3)
    ring_two(2)
    pg.three()
    ring_two(3)
    for place in ("O", "Y", "L", "R", "LY", "RY", "D", "DY"):
        pg.pair(place)
    ring_three(0)
    project(0)
    ring_three(1)
    project(1)
    ring_three(2)
    project(2)

    def text_moved(i, carry):
        @pl.when(jnp.logical_not(jnp.logical_and(2 * h + i % 2 == s, i // 2 == h)))
        def _():
            remote(tpart.at[0], tpart_in.at[i % 2, i // 2], osend.at[0], orecv.at[i % 2, i // 2],
                   partner).wait_recv()
        return carry

    lax.fori_loop(0, 16, text_moved, 0)

    @pl.when(home == 1)
    def _():
        pltpu.make_async_copy(tpart.at[0], tpart_in.at[c, h], own_sem.at[3]).wait()

    out_cols = pl.ds(pl.multiple_of(h * PART, PART), PART)
    sums = jnp.concatenate([jnp.sum(tpart_in[0], axis=0), jnp.sum(tpart_in[1], axis=0)], axis=1)
    text_out[...] = (txt[:, out_cols].astype(F32) + modt[pl.ds(2, 1), out_cols] * sums).astype(BF)

    ring_three(3)
    project(3)
    gate = modv[pl.ds(2, 1), out_cols]

    def write(i, carry):
        rows = pl.ds(pl.multiple_of(i * 16, 16), 16)
        at = pl.ds(pl.multiple_of(((i % TILES) * 8 + i // TILES) * 16, 16), 16)
        video_out[rows, :] = (vid[rows, out_cols].astype(F32) + gate * acc2[at, :]).astype(BF)
        return carry

    lax.fori_loop(0, 40, write, 0, unroll=4)

    def left_t(d, carry):
        remote(nt.at[0], tnt.at[0], tsend.at[d], trecv.at[d], partner).wait_send()
        remote(ts.at[0], ts_in.at[0], msend.at[d], mrecv.at[d], partner).wait_send()
        remote(atg.at[0], atg.at[0], asend.at[d], arecv.at[d], partner).wait_send()
        return carry

    lax.fori_loop(1, 16, left_t, 0)

    def left_w(j, carry):
        @pl.when(jnp.logical_not(jnp.logical_and(2 * j + c == s, s // 2 == h)))
        def _():
            remote(pv.at[:, 0], wp.at[0, 0, 0], wsend.at[j], wrecv.at[0], partner).wait_send()
        return carry

    lax.fori_loop(0, 8, left_w, 0)

    def left_o(i, carry):
        @pl.when(jnp.logical_not(jnp.logical_and(i == s, s // 2 == h)))
        def _():
            remote(tpart.at[0], tpart_in.at[0, 0], osend.at[i], orecv.at[0, 0], partner).wait_send()
        return carry

    lax.fori_loop(0, 16, left_o, 0)
    for cp in sent:
        cp.wait_send()


def block_kernel(vid, txt, modv, modt, w, wt, pv, pt, gainv, gaint, windows, text_len):
    vm = pl.BlockSpec(memory_space=pltpu.VMEM)
    sm = pl.BlockSpec(memory_space=pltpu.SMEM)
    hbm = pl.BlockSpec(memory_space=pl.ANY)
    dma = pltpu.SemaphoreType.DMA
    v = pltpu.VMEM
    return pl.pallas_call(
        kernel,
        name="attention_block",
        out_shape=(jax.ShapeDtypeStruct((ROWS, PART), BF), jax.ShapeDtypeStruct((16, PART), BF)),
        in_specs=[hbm] + [vm] * 3 + [hbm] * 4 + [vm] * 2 + [sm, sm],
        out_specs=(vm, vm),
        scratch_shapes=[
            v((ROWS, 3072), BF), v((3, SHARD, PART), BF), v((SHARD, PART), BF), v((SHARD, PART), BF),
            v((3, 8, 16, SHARD), BF),
            v((ROWS, 3072), BF), v((3, 8, 2, 3, SHARD, HD), BF), v((3, ROWS, PART), F32),
            v((16, 16, SHARD), BF), v((16, 16, SHARD), BF),
            v((2, 8, 16, WIDE), F32), v((8, 16, WIDE), F32), v((8, 16, WIDE), F32),
            v((16, 16, WIDE), BF),
            v((3, ROWS, HD), BF), v((3, ROWS, 2 * HD), BF), v((5, 3, ROWS, 2 * HD), BF),
            v((3, ROWS, HD), F32), v((3, ROWS, 2 * HD), F32), v((8, 3, ROWS, HD), BF),
            v((8, 2, 8, 3, 16, SHARD), BF), v((ROWS, PART), F32),
            v((16, 16, 512), BF), v((16, 16, 512), BF), v((16, 16, PART), BF),
            v((16, 16, SHARD), F32), v((2, 8, 16, SHARD), F32),
            dma((11,)), dma((3, 19)), dma((3, 19)), dma((16,)), dma((16,)),
            dma((8,)), dma((8,)), dma((15,)), dma((15,)),
            dma((5, 3)), dma((5, 3)), dma((9, 4)), dma((9, 4)),
            dma((8,)), dma((8,)), dma((19,)), dma((19,)),
            dma((16,)), dma((16,)), dma((16,)), dma((16,)), dma((16,)), dma((2, 8)),
        ],
        compiler_params=pltpu.CompilerParams(
            collective_id=1, has_side_effects=True, vmem_limit_bytes=58 * 2**20),
    )(vid, txt, modv, modt, w, wt, pv, pt, gainv, gaint, windows, text_len)


def body(video_in, text_in, mod_video, mod_text, qkv_video, qkv_text, proj_video, proj_text,
         gain_video, gain_text, windows, text_len):
    return block_kernel(
        video_in, text_in, mod_video, mod_text,
        jnp.transpose(qkv_video, (1, 0, 2)), jnp.transpose(qkv_text, (1, 0, 2)),
        proj_video.T, proj_text.T,
        gain_video, gain_text, windows.T, text_len)


def solution(mesh):
    return jax.shard_map(
        body,
        mesh=mesh,
        in_specs=(
            P("seq", None), P("seq", None), P(), P(),
            P("seq", None, "head"), P("seq", None, "head"),
            P("head", "seq"), P("head", "seq"), P(), P(), P(), P(),
        ),
        out_specs=(P("seq", "head"), P("seq", "head")),
        check_vma=False,
    )
```
